128 devices in a mesh: slab: 8 (over x_lo, z), piece: 16 (over y, x_hi, core).
Axes of the slice: x: 4 (x_hi: 2, x_lo: 2; x = x_hi * 2 + x_lo), y: 4, z: 4, core: 2. Of those that a mesh axis runs over, the one named last changes fastest.
Arguments:
- fine_tiles: bfloat16 [1024, 64, 512], P(('slab', 'piece')), may hold values from -0.25 to 0.25
- fine_cols: int32 [1024, 8], P(('slab', 'piece')), may hold values from 0 to 23
- bond_mask: int32 [1024, 8], P(('slab', 'piece')), may hold values 0 or 1
- diag_inv: bfloat16 [1024, 64, 64], P(('slab', 'piece')), may hold values from -0.75 to 0.75
- tentative: bfloat16 [1024, 64, 64], P(('slab', 'piece')), may hold values from -0.75 to 0.75
- aggregate: int32 [1024], P(('slab', 'piece')), may hold values from 0 to 7
- tentative_two: bfloat16 [1024, 64, 64], P(('slab', 'piece')), may hold values from -0.75 to 0.75
- aggregate_two: int32 [1024], P(('slab', 'piece')), may hold values from 0 to 15
Outputs:
- coarse_one: float32 [1024, 64, 3584], P(('slab', 'piece'))
- coarse_two: float32 [128, 64, 7168], P(('slab', 'piece'))
The draws below stay inside these ranges and needn't reach their ends.
All inputs are finite; a program needn't handle non-finite values. No bound on the sum of `bond_mask` on one device may be relied on, other than what follows from the above.
Results may differ from the reference program's by a relative error of at most 0.008.
Values may be sent and summed in bfloat16 or wider, within the bound.
No kernel may reach another device: no remote copies, remote signals or barrier semaphores. Data moves between devices by JAX's collectives and lax.ppermute only.
A program may use at most 128 MiB of HBM per device.

```python
import jax
import jax.numpy as jnp
from jax import lax

TILE = 64
BLOCKS = 8
SLOTS = 8
AGGS = 8
FINE_ROWS = 1024
AGG_ROWS = 1024
TWO_SLAB = 16
N_SLAB = 8
N_PIECE = 16
DEVICES = 128


def plant(result, stream_key, low, top_value):
    index_at = [jax.random.randint(jax.random.fold_in(stream_key, axis), (), 0, length) for axis, length in enumerate(result.shape)]
    widest = result.shape.index(max(result.shape))
    beside = index_at[:widest] + [(index_at[widest] + 1) % result.shape[widest]] + index_at[widest + 1:]
    return result.at[tuple(index_at)].set(low).at[tuple(beside)].set(top_value)


def shard_levels(rng, dims, cuts, smallest, top_value):
    def one(dim, parts):
        draws = jax.random.uniform(jax.random.fold_in(jax.random.fold_in(rng, 6), dim), (parts,), jnp.float32, smallest / len(cuts), top_value / len(cuts))
        return jnp.repeat(jnp.exp(draws), dims[dim] // parts).reshape((-1,) + (1,) * (len(dims) - dim - 1))

    gain = one(*cuts[0])
    for cut in cuts[1:]:
        gain = gain * one(*cut)
    return gain


def scatter_about(rng, dims, scale, bound, split=(), held_as=jnp.bfloat16):
    array = jax.random.normal(rng, dims, jnp.float32) * scale
    if len(split) > 0:
        array = shard_levels(rng, dims, split, -0.22, 0.18) * array
    return jnp.clip(array, min=-bound, max=bound).astype(held_as)


def setup_inputs(seed: int = 0) -> dict:
    keys = jax.random.split(jax.random.key(seed), 9)
    return {
        "fine_tiles": scatter_about(keys[0], (FINE_ROWS, TILE, SLOTS * TILE), (TILE * SLOTS) ** -0.5, 0.25, ((0, 128),)),
        "fine_cols": plant(jax.random.randint(keys[1], (FINE_ROWS, SLOTS), 0, 3 * BLOCKS), jax.random.fold_in(keys[1], 1), 0, (3 * BLOCKS) - 1).astype(jnp.int32),
        "bond_mask": plant((jax.random.randint(keys[2], (FINE_ROWS, SLOTS), 0, 8) < 7).astype(jnp.int32), jax.random.fold_in(keys[2], 1), 0, 1),
        "diag_inv": scatter_about(keys[3], (FINE_ROWS, TILE, TILE), TILE ** -0.5, 0.75, ((0, 128),)),
        "tentative": scatter_about(keys[4], (FINE_ROWS, TILE, TILE), TILE ** -0.5, 0.75, ((0, 128),)),
        "aggregate": plant(jax.random.randint(keys[5], (FINE_ROWS,), 0, AGGS), jax.random.fold_in(keys[5], 1), 0, AGGS - 1).astype(jnp.int32),
        "tentative_two": scatter_about(keys[6], (AGG_ROWS, TILE, TILE), TILE ** -0.5, 0.75, ((0, 128),)),
        "aggregate_two": plant(jax.random.randint(keys[7], (AGG_ROWS,), 0, TWO_SLAB), jax.random.fold_in(keys[7], 1), 0, TWO_SLAB - 1).astype(jnp.int32),
    }


DAMPING = 2.0 / 3.0
EXACT_MODE = lax.Precision.HIGHEST


def slot_tiles(tiles, agg_ids, count):
    onehot = (agg_ids[:, None] == jnp.arange(count, dtype=jnp.int32)[None, :]).astype(jnp.float32)
    placed = tiles.astype(jnp.float32)[:, :, None, :] * onehot[:, None, :, None]
    return placed.astype(jnp.bfloat16).reshape(tiles.shape[0], tiles.shape[1], count * tiles.shape[2])


def prolong_rows(fine_tiles, fine_cols, bond_mask, diag_inv, own_slot, basis_rim):
    blocks, tile_size = diag_inv.shape[0], diag_inv.shape[1]
    slot_count = fine_cols.shape[1]
    agg_width = own_slot.shape[2]
    quad = fine_tiles.astype(jnp.float32).reshape(blocks, tile_size, slot_count, tile_size)
    smooth = jnp.einsum('irs,iskt->ikrt', diag_inv.astype(jnp.float32), quad, precision=EXACT_MODE)
    smooth = (DAMPING * bond_mask.astype(jnp.float32)[:, :, None, None] * smooth).astype(jnp.bfloat16)
    summed = jnp.zeros((blocks, tile_size, 3, agg_width), jnp.float32)
    for k in range(slot_count):
        column = fine_cols[:, k].astype(jnp.int32)
        rows_in = jnp.take(basis_rim, column, axis=0).astype(jnp.float32)
        product = jnp.einsum('irs,isq->irq', smooth[:, k].astype(jnp.float32), rows_in, precision=EXACT_MODE)
        side_mask = (column[:, None] // blocks == jnp.arange(3, dtype=jnp.int32)[None, :]).astype(jnp.float32)
        summed = summed - product[:, :, None, :] * side_mask[:, None, :, None]
    summed = summed.at[:, :, 1, :].add(own_slot.astype(jnp.float32))
    return summed.reshape(blocks, tile_size, 3 * agg_width).astype(jnp.bfloat16)


def apply_rows(fine_tiles, fine_cols, bond_mask, prolong_rim, agg_width):
    blocks, tile_size = fine_tiles.shape[0], fine_tiles.shape[1]
    slot_count = fine_cols.shape[1]
    quad = fine_tiles.astype(jnp.float32).reshape(blocks, tile_size, slot_count, tile_size)
    quad = quad * bond_mask.astype(jnp.float32)[:, None, :, None]
    sides = jnp.zeros((blocks, tile_size, 3, 3 * agg_width), jnp.float32)
    for k in range(slot_count):
        column = fine_cols[:, k].astype(jnp.int32)
        rows_in = jnp.take(prolong_rim, column, axis=0).astype(jnp.float32)
        product = jnp.einsum('irs,isq->irq', quad[:, :, k, :], rows_in, precision=EXACT_MODE)
        side_mask = (column[:, None] // blocks == jnp.arange(3, dtype=jnp.int32)[None, :]).astype(jnp.float32)
        sides = sides + product[:, :, None, :] * side_mask[:, None, :, None]
    summed = jnp.pad(sides[:, :, 0], ((0, 0), (0, 0), (0, 2 * agg_width)))
    summed = summed + jnp.pad(sides[:, :, 1], ((0, 0), (0, 0), (agg_width, agg_width)))
    summed = summed + jnp.pad(sides[:, :, 2], ((0, 0), (0, 0), (2 * agg_width, 0)))
    return summed.astype(jnp.bfloat16)


def level_partial(coarse_rows, two_tiles, two_ids, basis, groups):
    agg_count, tile_size = two_tiles.shape[0], two_tiles.shape[1]
    left = jnp.einsum('ars,arc->asc', two_tiles.astype(jnp.float32), coarse_rows, precision=EXACT_MODE)
    left = left.reshape(agg_count, tile_size, 7, agg_count, tile_size)
    right = basis.astype(jnp.float32).reshape(7, agg_count, tile_size, groups * tile_size)
    both = jnp.einsum('asobt,obtq->asoq', left, right, precision=EXACT_MODE)
    onehot = (two_ids[:, None] == jnp.arange(groups, dtype=jnp.int32)[None, :]).astype(jnp.float32)
    placed = jnp.einsum('ag,asoq->gsoq', onehot, both, precision=EXACT_MODE)
    return placed.reshape(groups, tile_size, 7 * groups * tile_size)


def reference(fine_tiles, fine_cols, bond_mask, diag_inv, tentative, aggregate, tentative_two, aggregate_two):
    slabs, groups = N_SLAB, N_PIECE
    agg_width = AGGS * TILE

    def on_grid(x, count):
        return x.reshape((slabs, groups, count) + x.shape[1:])

    def framed(x, count, depth):
        grid = on_grid(x, count)
        zero = jnp.zeros((depth,) + grid.shape[1:], grid.dtype)
        return jnp.concatenate([zero, grid, zero], 0)

    tiles_g = on_grid(fine_tiles, BLOCKS)
    cols_g = on_grid(fine_cols, BLOCKS)
    mask_g = on_grid(bond_mask, BLOCKS)
    dinv_g = on_grid(diag_inv, BLOCKS)
    qslot = slot_tiles(tentative, aggregate, AGGS)
    qslot_g = on_grid(qslot, BLOCKS)
    qpad = framed(qslot, BLOCKS, 1)

    def first(index):
        s = index // groups
        p = index % groups
        rim = jnp.concatenate([qpad[s, p], qpad[s + 1, p], qpad[s + 2, p]], 0)
        return prolong_rows(tiles_g[s, p], cols_g[s, p], mask_g[s, p], dinv_g[s, p], qslot_g[s, p], rim)

    device_ids = jnp.arange(DEVICES, dtype=jnp.int32)
    prolong = lax.map(first, device_ids)
    prolong_flat = prolong.reshape(DEVICES * BLOCKS, TILE, 3 * agg_width)
    ppad = framed(prolong_flat, BLOCKS, 1)

    def second(index):
        s = index // groups
        p = index % groups
        rim = jnp.concatenate([ppad[s, p], ppad[s + 1, p], ppad[s + 2, p]], 0)
        applied = apply_rows(tiles_g[s, p], cols_g[s, p], mask_g[s, p], rim, agg_width)
        own = prolong[index].astype(jnp.float32).reshape(BLOCKS * TILE, 3 * agg_width)
        right = applied.astype(jnp.float32).reshape(BLOCKS * TILE, 5 * agg_width)
        product = lax.dot_general(own, right, (((0,), (0,)), ((), ())), precision=EXACT_MODE)
        return product.reshape(3, AGGS, TILE, 5 * agg_width)

    rowsets = lax.map(second, device_ids).reshape(slabs, groups, 3, AGGS, TILE, 5 * agg_width)
    zero_slab = jnp.zeros((1, groups, AGGS, TILE, 5 * agg_width), jnp.float32)
    from_next = jnp.concatenate([rowsets[1:, :, 0], zero_slab], 0)
    from_prev = jnp.concatenate([zero_slab, rowsets[:-1, :, 2]], 0)
    coarse = jnp.pad(rowsets[:, :, 1], ((0, 0), (0, 0), (0, 0), (0, 0), (agg_width, agg_width)))
    coarse = coarse + jnp.pad(from_next, ((0, 0), (0, 0), (0, 0), (0, 0), (2 * agg_width, 0)))
    coarse = coarse + jnp.pad(from_prev, ((0, 0), (0, 0), (0, 0), (0, 0), (0, 2 * agg_width)))
    coarse_one = coarse.reshape(DEVICES * AGGS, TILE, 7 * agg_width)

    q2slot = slot_tiles(tentative_two, aggregate_two, groups)
    q2pad = framed(q2slot, AGGS, 3)
    two_g = on_grid(tentative_two, AGGS)
    ids_g = on_grid(aggregate_two, AGGS)

    def slab_sum(s):
        def add_piece(p, summed):
            basis = jnp.concatenate([q2pad[s + j, p] for j in range(7)], 0)
            term = level_partial(coarse[s, p], two_g[s, p], ids_g[s, p], basis, groups)
            term = lax.optimization_barrier(term.astype(jnp.bfloat16)).astype(jnp.float32)
            return summed + term

        start = jnp.zeros((groups, TILE, 7 * groups * TILE), jnp.float32)
        return lax.fori_loop(0, groups, add_piece, start)

    level_two = lax.map(slab_sum, jnp.arange(slabs, dtype=jnp.int32))
    coarse_two = level_two.reshape(slabs * groups, TILE, 7 * groups * TILE)
    return (coarse_one, coarse_two)
```

```python
import functools

import jax
import jax.numpy as jnp
from jax import lax
from jax.experimental import pallas as pl
from jax.experimental.pallas import tpu as pltpu
from jax.sharding import PartitionSpec as P

DAMPING = 2.0 / 3.0
TILE = 64
N = 8
W = N * TILE
LANES = 128
TRASH = 3 * N
WIDE = 3 * W + LANES
ROW_D, ROW_Q, ROW_T, ROW_META, ROWS = W, W + 64, W + 128, W + 192, W + 208
VMEM = pl.BlockSpec(memory_space=pltpu.VMEM)
BF16, F32, I32 = jnp.bfloat16, jnp.float32, jnp.int32
GROUPS = 16
PART = 4
CHUNK = N * PART
TERM_W = 7 * W + LANES
DENSE = 7 * GROUPS * TILE
QUARTER = DENSE // 4


def params():
    return pltpu.CompilerParams(vmem_limit_bytes=62 << 20)


def dot(a, b):
    return jnp.dot(a, b, preferred_element_type=F32)


def iota(shape, dim):
    return lax.broadcasted_iota(I32, shape, dim)


def pack_kernel(a_ref, d_ref, q_ref, t_ref, cols_ref, mask_ref, agg_ref, agg2_ref, out_ref, meta):
    for i in range(N):
        out_ref[i * TILE:(i + 1) * TILE, :] = a_ref[i]
    for row, ref in ((ROW_D, d_ref), (ROW_Q, q_ref), (ROW_T, t_ref)):
        for w in range(N // 2):
            pair = jnp.concatenate([ref[2 * w], ref[2 * w + 1]], axis=1)
            out_ref[row:row + TILE, w * LANES:(w + 1) * LANES] = pair
    meta[...] = jnp.zeros_like(meta)
    meta[0:8, 0:8] = jnp.where(mask_ref[...] > 0, cols_ref[...], TRASH).astype(F32)
    meta[8:9, 0:8] = agg_ref[...].astype(F32)
    meta[9:10, 0:8] = agg2_ref[...].astype(F32)
    out_ref[ROW_META:ROWS, :] = meta[...].astype(BF16)


def pack(a, d, q, t, cols, mask, agg, agg2):
    return pl.pallas_call(
        pack_kernel,
        out_shape=jax.ShapeDtypeStruct((ROWS, W), BF16),
        in_specs=[VMEM] * 8,
        out_specs=VMEM,
        scratch_shapes=[pltpu.VMEM((16, W), F32)],
        compiler_params=params(),
    )(a, d, q, t, cols, mask, agg.reshape(1, N), agg2.reshape(1, N))


def halves(x):
    high = iota(x.shape, 1) >= TILE
    swapped = jnp.concatenate([x[:, TILE:], x[:, :TILE]], axis=1)
    zero = jnp.zeros_like(x)
    return (
        (jnp.where(high, zero, x), jnp.where(high, swapped, zero)),
        (jnp.where(high, zero, swapped), jnp.where(high, x, zero)),
    )


def window(index):
    return pl.ds(pl.multiple_of((index // 2) * LANES, LANES), LANES)


def pick(variants, index):
    return jnp.where(index % 2 == 1, variants[1], variants[0])


def block_diagonal(row):
    block = iota(row.shape, 1) // TILE
    zero = jnp.zeros_like(row)
    return jnp.concatenate([jnp.where(block == i, row, zero) for i in range(N)], axis=0)


def to_scalars(pairs, sem):
    copies = [pltpu.make_async_copy(v, s, sem.at[n]) for n, (v, s) in enumerate(pairs)]
    for c in copies:
        c.start()
    for c in copies:
        c.wait()


def level_kernel(m3, m2, m1, own, p1, p2, p3, c_ref, term_ref,
                 ad, sm, qs, pr, ra, tpt, meta_v, meta_s, ids_v, sem):
    near = (m2, m1, own, p1, p2)
    wide = (m3, m2, m1, own, p1, p2, p3)
    base = tuple(0 if r.shape[0] == ROWS else ROW_Q for r in wide)
    for n, ref in enumerate(wide):
        top = ROW_META - base[n]
        meta_v[n] = ref[top:top + 16, 0:LANES].astype(F32).astype(I32)
    to_scalars([(meta_v.at[n], meta_s.at[n]) for n in range(7)], sem)

    for n, ref in enumerate(wide):
        qs[n] = jnp.zeros((W, W), BF16)
        top = ROW_Q - base[n]
        for w in range(N // 2):
            sides = halves(ref[top:top + TILE, w * LANES:(w + 1) * LANES])
            for h in range(2):
                c = 2 * w + h
                g = meta_s[n, 8, c]
                qs[n, c * TILE:(c + 1) * TILE, window(g)] = pick(sides[h], g)

    for t, ref in enumerate(near):
        def place_row(i, carry, t=t, ref=ref):
            rows = pl.ds(pl.multiple_of(i * TILE, TILE), TILE)
            ad[t, rows, :] = jnp.zeros((TILE, WIDE), BF16)
            for w in range(N // 2):
                sides = halves(ref[rows, w * LANES:(w + 1) * LANES])
                for h in range(2):
                    c = meta_s[t + 1, i, 2 * w + h]
                    ad[t, rows, window(c)] = ad[t, rows, window(c)] + pick(sides[h], c)
            return carry

        lax.fori_loop(0, N, place_row, 0)
        for w in range(N // 2):
            pair = ref[ROW_D:ROW_D + TILE, w * LANES:(w + 1) * LANES]
            high = iota(pair.shape, 1) >= TILE
            zero = jnp.zeros_like(pair)
            diag = jnp.concatenate([jnp.where(high, zero, pair), jnp.where(high, pair, zero)], axis=0)
            rows = slice(w * LANES, (w + 1) * LANES)
            sm[t, rows, :] = (DAMPING * dot(diag, ad[t, rows, 0:3 * W])).astype(BF16)

    def prolong(t, carry):
        for j in range(3):
            block = -dot(sm[t, :, j * W:(j + 1) * W], qs[t + j])
            if j == 1:
                block = qs[t + 1].astype(F32) + block
            pr[t, :, j * W:(j + 1) * W] = block.astype(BF16)
        return carry

    lax.fori_loop(0, 5, prolong, 0)

    turned = [pr[t, :, (3 - t) * W:(4 - t) * W].T for t in (1, 2, 3)]
    for f in range(5):
        total = None
        for t in (1, 2, 3):
            j = f - t + 1
            if 0 <= j < 3:
                part = dot(turned[t - 1], ad[t, :, j * W:(j + 1) * W])
                total = part if total is None else total + part
        ra[:, f * W:(f + 1) * W] = total.astype(BF16)

    def coarse(o, fs):
        total = None
        for f in fs:
            part = dot(ra[:, pl.ds(pl.multiple_of(f * W, W), W)],
                       pr[f, :, pl.ds(pl.multiple_of((o - f) * W, W), W)])
            total = part if total is None else total + part
        c_ref[:, pl.ds(pl.multiple_of(o * W, W), W)] = total

    coarse(0, (0,))
    coarse(1, (0, 1))

    def middle(o, carry):
        coarse(o, (o - 2, o - 1, o))
        return carry

    lax.fori_loop(2, 5, middle, 0)
    coarse(5, (3, 4))
    coarse(6, (4,))

    here = ROW_T
    left = block_diagonal(own[here:here + TILE, :])
    lead = iota((W, W), 0)
    target = ((lead >> 2) & 7) * TILE + (lead >> 5) * PART + (lead & 3)
    turn = (target == iota((W, W), 1)).astype(F32).astype(BF16)
    tpt[...] = lax.dot_general(turn, left, (((1,), (1,)), ((), ())), preferred_element_type=F32).astype(BF16)
    ids_v[...] = jnp.zeros_like(ids_v)
    for n, ref in enumerate(wide):
        lhs = dot(tpt[...], c_ref[:, n * W:(n + 1) * W].astype(BF16)).astype(BF16)
        top = ROW_T - base[n]
        for w in range(N // 2):
            pair = ref[top:top + TILE, w * LANES:(w + 1) * LANES]
            high = iota(pair.shape, 1) >= TILE
            zero = jnp.zeros_like(pair)
            diag = jnp.concatenate([jnp.where(high, zero, pair), jnp.where(high, pair, zero)], axis=0)
            at = n * W + w * LANES
            term_ref[:, at:at + LANES] = dot(lhs[:, w * LANES:(w + 1) * LANES], diag).astype(BF16)
        ids_v[n:n + 1, :] = meta_v[n, 9:10, :].astype(F32)
    for q in range(GROUPS):
        term_ref[q * CHUNK:(q + 1) * CHUNK, 7 * W:TERM_W] = ids_v[...].astype(BF16)


def levels(*bufs):
    return pl.pallas_call(
        level_kernel,
        out_shape=(jax.ShapeDtypeStruct((W, 7 * W), F32), jax.ShapeDtypeStruct((W, TERM_W), BF16)),
        in_specs=[VMEM] * 7,
        out_specs=(VMEM, VMEM),
        scratch_shapes=[
            pltpu.VMEM((5, W, WIDE), BF16),
            pltpu.VMEM((5, W, 3 * W), BF16),
            pltpu.VMEM((7, W, W), BF16),
            pltpu.VMEM((5, W, 3 * W), BF16),
            pltpu.VMEM((W, 5 * W), BF16),
            pltpu.VMEM((W, W), BF16),
            pltpu.VMEM((7, 16, LANES), I32),
            pltpu.SMEM((7, 16, LANES), I32),
            pltpu.VMEM((CHUNK, LANES), F32),
            pltpu.SemaphoreType.DMA((7,)),
        ],
        compiler_params=params(),
    )(*bufs)


def merge_kernel(x_ref, out_ref, y, ids_v, ids_s, sem):
    for p in range(GROUPS):
        ids_v[p] = x_ref[p, 0:16, 7 * W:TERM_W].astype(F32).astype(I32)
    to_scalars([(ids_v, ids_s)], sem)
    y[...] = jnp.zeros_like(y)

    def one(n, carry):
        p, o = n // 7, n % 7
        rows = pl.ds(pl.multiple_of(p * CHUNK, CHUNK), CHUNK)
        for w in range(N // 2):
            at = pl.ds(pl.multiple_of(o * W + w * LANES, LANES), LANES)
            sides = halves(x_ref[p, :, at])
            for h in range(2):
                g = ids_s[p, o, 2 * w + h]
                cols = pl.ds(pl.multiple_of(o * GROUPS * TILE + (g // 2) * LANES, LANES), LANES)
                y[rows, cols] = y[rows, cols] + pick(sides[h], g)
        return carry

    lax.fori_loop(0, GROUPS * 7, one, 0)

    groups = jnp.concatenate([ids_v[p, 3:4, :] for p in range(GROUPS)], axis=0).astype(F32).astype(BF16)
    spread = (((iota((LANES, W), 1) >> 2) & 7) == iota((LANES, W), 0)).astype(F32).astype(BF16)
    each = dot(groups, spread)
    mine = (iota((GROUPS, W), 1) >> 5) == iota((GROUPS, W), 0)
    group = jnp.sum(jnp.where(mine, each, 0.0), axis=0, keepdims=True).astype(I32)
    row, col = iota((256, W), 0), iota((256, W), 1)
    hit = ((row >> 4) == group) & ((row & 3) == (col & 3))
    total = None
    for cq in range(4):
        take = (hit & (((row >> 2) & 3) == cq)).astype(F32).astype(BF16)
        part = dot(take, y[:, cq * QUARTER:(cq + 1) * QUARTER])
        total = part if total is None else total + part
    out_ref[...] = total.astype(BF16)


def merge(x):
    return pl.pallas_call(
        merge_kernel,
        out_shape=jax.ShapeDtypeStruct((256, QUARTER), BF16),
        in_specs=[VMEM],
        out_specs=VMEM,
        scratch_shapes=[
            pltpu.VMEM((GROUPS * CHUNK, DENSE), BF16),
            pltpu.VMEM((GROUPS, 16, LANES), I32),
            pltpu.SMEM((GROUPS, 16, LANES), I32),
            pltpu.SemaphoreType.DMA((1,)),
        ],
        compiler_params=params(),
    )(x)


def finish_kernel(x_ref, out_ref):
    row, col = iota((TILE, 256), 0), iota((TILE, 256), 1)
    same = ((row >> 2) == (col >> 4)) & ((row & 3) == (col & 3))
    for cq in range(4):
        take = (same & (((col >> 2) & 3) == cq)).astype(F32).astype(BF16)
        out_ref[0, :, cq * QUARTER:(cq + 1) * QUARTER] = dot(take, x_ref[...])


def finish(x):
    return pl.pallas_call(
        finish_kernel,
        out_shape=jax.ShapeDtypeStruct((1, TILE, DENSE), F32),
        in_specs=[VMEM],
        out_specs=VMEM,
        compiler_params=params(),
    )(x)


def along(block, step):
    count = lax.axis_size("slab")
    route = [(i, i + step) for i in range(count) if 0 <= i + step < count]
    return lax.ppermute(block, "slab", route)


def per_device(fine_tiles, fine_cols, bond_mask, diag_inv, tentative, aggregate, tentative_two, aggregate_two):
    own = pack(fine_tiles, diag_inv, tentative, tentative_two, fine_cols, bond_mask, aggregate, aggregate_two)
    m1, p1 = along(own, 1), along(own, -1)
    m2, p2 = along(m1, 1), along(p1, -1)
    m3, p3 = along(m2[ROW_Q:], 1), along(p2[ROW_Q:], -1)
    coarse, term = levels(m3, m2, m1, own, p1, p2, p3)
    got = lax.all_to_all(term.reshape(GROUPS, CHUNK, TERM_W), "piece", 0, 0)
    dense = merge(got)
    back = lax.all_to_all(dense.reshape(GROUPS, 16, QUARTER), "piece", 0, 0)
    level_two = finish(back.reshape(256, QUARTER))
    return coarse.reshape(N, TILE, 7 * W), level_two


def solution(mesh):
    both = ("slab", "piece")
    placed = (
        P(both, None, None), P(both, None), P(both, None), P(both, None, None),
        P(both, None, None), P(both), P(both, None, None), P(both),
    )
    return jax.shard_map(
        per_device,
        mesh=mesh,
        in_specs=placed,
        out_specs=(P(both, None, None), P(both, None, None)),
        check_vma=False,
    )
```

```python
import functools

import jax
import jax.numpy as jnp
from jax import lax
from jax.experimental import pallas as pl
from jax.experimental.pallas import tpu as pltpu
from jax.sharding import PartitionSpec as P

DAMPING = 2.0 / 3.0
TILE = 64
N = 8
W = N * TILE
LANES = 128
TRASH = 3 * N
WIDE = 3 * W + LANES
ROW_D, ROW_Q, ROW_T, ROW_META, ROWS = W, W + 64, W + 128, W + 192, W + 208
ANY = pl.BlockSpec(memory_space=pl.ANY)
VMEM = pl.BlockSpec(memory_space=pltpu.VMEM)
BF16, F32, I32 = jnp.bfloat16, jnp.float32, jnp.int32
GROUPS = 16
PART = 4
CHUNK = N * PART
DENSE = 7 * GROUPS * TILE
QUARTER = GROUPS * TILE // 4
TAIL = pl.BlockSpec((144, W), lambda i: (ROW_Q // 144, 0))
TAIL_Q, TAIL_T, TAIL_META = 0, 64, 128


def params():
    return pltpu.CompilerParams(vmem_limit_bytes=62 << 20)


def dot(a, b):
    return jnp.dot(a, b, preferred_element_type=F32)


def iota(shape, dim):
    return lax.broadcasted_iota(I32, shape, dim)


def pack_kernel(a_ref, d_ref, q_ref, t_ref, cols_ref, mask_ref, agg_ref, agg2_ref, out_ref, meta):
    for i in range(N):
        out_ref[i * TILE:(i + 1) * TILE, :] = a_ref[i]
    for row, ref in ((ROW_D, d_ref), (ROW_Q, q_ref), (ROW_T, t_ref)):
        for w in range(N // 2):
            pair = jnp.concatenate([ref[2 * w], ref[2 * w + 1]], axis=1)
            out_ref[row:row + TILE, w * LANES:(w + 1) * LANES] = pair
    meta[...] = jnp.zeros_like(meta)
    meta[0:8, 0:8] = jnp.where(mask_ref[...] > 0, cols_ref[...], TRASH).astype(F32)
    meta[8:9, 0:8] = agg_ref[...].astype(F32)
    meta[9:10, 0:8] = agg2_ref[...].astype(F32)
    out_ref[ROW_META:ROWS, :] = meta[...].astype(BF16)


def pack(a, d, q, t, cols, mask, agg, agg2):
    return pl.pallas_call(
        pack_kernel,
        out_shape=jax.ShapeDtypeStruct((ROWS, W), BF16),
        in_specs=[VMEM] * 8,
        out_specs=VMEM,
        scratch_shapes=[pltpu.VMEM((16, W), F32)],
        compiler_params=params(),
    )(a, d, q, t, cols, mask, agg.reshape(1, N), agg2.reshape(1, N))


def halves(x):
    high = iota(x.shape, 1) >= TILE
    swapped = jnp.concatenate([x[:, TILE:], x[:, :TILE]], axis=1)
    zero = jnp.zeros_like(x)
    return (
        (jnp.where(high, zero, x), jnp.where(high, swapped, zero)),
        (jnp.where(high, zero, swapped), jnp.where(high, x, zero)),
    )


def window(index):
    return pl.ds(pl.multiple_of((index // 2) * LANES, LANES), LANES)


def pick(variants, index):
    return jnp.where(index % 2 == 1, variants[1], variants[0])


def block_diagonal(row):
    block = iota(row.shape, 1) // TILE
    zero = jnp.zeros_like(row)
    return jnp.concatenate([jnp.where(block == i, row, zero) for i in range(N)], axis=0)


def to_scalars(pairs, sem):
    copies = [pltpu.make_async_copy(v, s, sem.at[n]) for n, (v, s) in enumerate(pairs)]
    for c in copies:
        c.start()
    for c in copies:
        c.wait()


def read_meta(tails, meta_v, meta_s, sem):
    for n, (ref, top) in enumerate(tails):
        meta_v[n] = ref[top:top + 16, 0:LANES].astype(F32).astype(I32)
    to_scalars([(meta_v.at[n], meta_s.at[n]) for n in range(len(tails))], sem)


def place_q(out, ref, top, meta_s, n):
    out[...] = jnp.zeros((W, W), BF16)
    for w in range(N // 2):
        sides = halves(ref[top:top + TILE, w * LANES:(w + 1) * LANES])
        for h in range(2):
            c = 2 * w + h
            g = meta_s[n, 8, c]
            out[c * TILE:(c + 1) * TILE, window(g)] = pick(sides[h], g)


def pair_diagonal(pair):
    high = iota(pair.shape, 1) >= TILE
    zero = jnp.zeros_like(pair)
    return jnp.concatenate([jnp.where(high, zero, pair), jnp.where(high, pair, zero)], axis=0)


def place_a(refs, outs, sms, meta_s, metas):
    def place_row(i, carry):
        rows = pl.ds(pl.multiple_of(i * TILE, TILE), TILE)
        for out in outs:
            out[rows, :] = jnp.zeros((TILE, WIDE), BF16)
        for w in range(N // 2):
            sides = [halves(ref[rows, w * LANES:(w + 1) * LANES]) for ref in refs]
            for h in range(2):
                for out, side, n in zip(outs, sides, metas):
                    c = meta_s[n, i, 2 * w + h]
                    out[rows, window(c)] = out[rows, window(c)] + pick(side[h], c)
        return carry

    lax.fori_loop(0, N, place_row, 0)

    def smooth(w, carry):
        rows = pl.ds(pl.multiple_of(w * LANES, LANES), LANES)
        for ref, out, sm in zip(refs, outs, sms):
            diag = pair_diagonal(ref[ROW_D:ROW_D + TILE, rows])
            sm[rows, :] = (DAMPING * dot(diag, out[rows, 0:3 * W])).astype(BF16)
        return carry

    lax.fori_loop(0, N // 2, smooth, 0)


def write_term(term, n, tpt, c, ref, top):
    lhs = dot(tpt[...], c.astype(BF16)).astype(BF16)
    for w in range(N // 2):
        diag = pair_diagonal(ref[top:top + TILE, w * LANES:(w + 1) * LANES])
        at = n * W + w * LANES
        term[:, at:at + LANES] = dot(lhs[:, w * LANES:(w + 1) * LANES], diag).astype(BF16)


def write_ids(term, count, ids_v, meta_v, order):
    ids_v[...] = jnp.zeros_like(ids_v)
    for row, n in enumerate(order):
        ids_v[row:row + 1, :] = meta_v[n, 9:10, :].astype(F32)
    for q in range(GROUPS):
        term[q * CHUNK:(q + 1) * CHUNK, count * W:] = ids_v[...].astype(BF16)


def block(j):
    return slice(j * W, (j + 1) * W)


def own_kernel(own, ad, sm, qs, r0, tpt, meta_v, meta_s, sem):
    read_meta([(own, ROW_META)], meta_v, meta_s, sem)
    place_q(qs, own, ROW_Q, meta_s, 0)
    place_a((own,), (ad,), (sm,), meta_s, (0,))
    r0[...] = (qs[...].astype(F32) - dot(sm[:, block(1)], qs[...])).astype(BF16)
    left = block_diagonal(own[ROW_T:ROW_T + TILE, :])
    lead = iota((W, W), 0)
    target = ((lead >> 2) & 7) * TILE + (lead >> 5) * PART + (lead & 3)
    turn = (target == iota((W, W), 1)).astype(F32).astype(BF16)
    tpt[...] = lax.dot_general(turn, left, (((1,), (1,)), ((), ())), preferred_element_type=F32).astype(BF16)


def start_own(own):
    shape = jax.ShapeDtypeStruct
    return pl.pallas_call(
        own_kernel,
        out_shape=(
            shape((W, WIDE), BF16), shape((W, 3 * W), BF16), shape((W, W), BF16),
            shape((W, W), BF16), shape((W, W), BF16),
        ),
        in_specs=[VMEM],
        out_specs=(VMEM,) * 5,
        scratch_shapes=[
            pltpu.VMEM((1, 16, LANES), I32),
            pltpu.SMEM((1, 16, LANES), I32),
            pltpu.SemaphoreType.DMA((1,)),
        ],
        compiler_params=params(),
        cost_estimate=pl.CostEstimate(flops=3_000_000_000, bytes_accessed=6 << 20, transcendentals=0),
    )(own)


def fetch(pairs, sem):
    copies = [pltpu.make_async_copy(src, dst, sem.at[n]) for n, (src, dst) in enumerate(pairs)]
    for c in copies:
        c.start()
    return copies


def near_kernel(m1, p1, ad_h, sm_h, qs_h, r0_h, tpt_h, own, c_ref, term_ref, part, ra_out, smo,
                ad0, ad1, ad2, sm0, sm1, sm2, qs0, qs1, qs2, rm, r0, rp, pw, tpt, ra, cbuf, tbuf,
                meta_v, meta_s, sem, in_sem, out_sem):
    ins = fetch(((qs_h, qs1), (r0_h, r0), (ad_h, ad1), (tpt_h, tpt), (sm_h, sm1)), in_sem)
    ads, sms, qss = (ad0, ad1, ad2), (sm0, sm1, sm2), (qs0, qs1, qs2)
    read_meta([(m1, ROW_META), (p1, ROW_META)], meta_v, meta_s, sem)
    place_q(qs0, m1, ROW_Q, meta_s, 0)
    place_q(qs2, p1, ROW_Q, meta_s, 1)
    place_a((m1, p1), (ad0, ad2), (sm0, sm2), meta_s, (0, 1))
    for copy in ins:
        copy.wait()

    rm[...] = (-dot(sm0[:, block(2)], qs1[...])).astype(BF16)
    rp[...] = (-dot(sm2[:, block(0)], qs1[...])).astype(BF16)
    turned = (rm[...].T, r0[...].T, rp[...].T)
    for f in range(5):
        total = None
        for t in range(3):
            if 0 <= f - t < 3:
                piece = dot(turned[t], ads[t][:, block(f - t)])
                total = piece if total is None else total + piece
        ra[:, block(f)] = total.astype(BF16)
    for n, f in enumerate((0, 1, 3, 4)):
        ra_out[:, block(n)] = ra[:, block(f)]
    smo[:, block(0)] = sm0[:, block(0)]
    smo[:, block(1)] = sm2[:, block(2)]

    cbuf[...] = dot(ra[:, block(1)], rm[...]) + dot(ra[:, block(2)], r0[...]) + dot(ra[:, block(3)], rp[...])
    out = pltpu.make_async_copy(cbuf, c_ref.at[:, block(3)], out_sem.at[0])
    out.start()
    write_term(tbuf, 0, tpt, cbuf[...], own, TAIL_T)
    sent = pltpu.make_async_copy(tbuf, term_ref.at[:, block(0)], out_sem.at[1])
    sent.start()

    for n, (t, f, g) in enumerate(((0, 1, 0), (2, 3, 2))):
        pw[...] = (qss[t][...].astype(F32) - dot(sms[t][:, block(1)], qss[t][...])).astype(BF16)
        known = dot(ra[:, block(f)], pw[...])
        pw[...] = (-dot(sm1[:, block(g)], qss[t][...])).astype(BF16)
        part[:, block(n)] = known + dot(ra[:, block(2)], pw[...])
    out.wait()
    sent.wait()


def near(m1, p1, ad, sm, qs, r0, tpt, own):
    shape = jax.ShapeDtypeStruct
    return pl.pallas_call(
        near_kernel,
        grid=(1,),
        out_shape=(
            shape((W, 7 * W), F32), shape((W, 3 * W + LANES), BF16), shape((W, 2 * W), F32),
            shape((W, 4 * W), BF16), shape((W, 2 * W), BF16),
        ),
        in_specs=[VMEM, VMEM] + [ANY] * 5 + [TAIL],
        out_specs=(ANY, ANY, VMEM, VMEM, VMEM),
        scratch_shapes=[pltpu.VMEM((W, WIDE), BF16)] * 3
        + [pltpu.VMEM((W, 3 * W), BF16)] * 3
        + [pltpu.VMEM((W, W), BF16)] * 8
        + [
            pltpu.VMEM((W, 5 * W), BF16),
            pltpu.VMEM((W, W), F32),
            pltpu.VMEM((W, W), BF16),
            pltpu.VMEM((2, 16, LANES), I32),
            pltpu.SMEM((2, 16, LANES), I32),
            pltpu.SemaphoreType.DMA((2,)),
            pltpu.SemaphoreType.DMA((5,)),
            pltpu.SemaphoreType.DMA((2,)),
        ],
        compiler_params=params(),
        cost_estimate=pl.CostEstimate(flops=9_000_000_000, bytes_accessed=14 << 20, transcendentals=0),
    )(m1, p1, ad, sm, qs, r0, tpt, own)


def second_kernel(m2, p2, m1, p1, own, m3, p3, part_h, ra_h, tpt_h, c_in, term_in, c_ref, term_ref, smm_out, smp_out,
                  flat, smm, smp, qs, pw, part, ra, tpt, cbuf, tbuf, meta_v, meta_s, ids_v, sem, in_sem, out_sem):
    del c_in, term_in, m3, p3
    ins = fetch(((part_h, part), (ra_h, ra), (tpt_h, tpt)), in_sem)
    read_meta([(m2, ROW_META), (p2, ROW_META), (m1, TAIL_META), (p1, TAIL_META), (own, TAIL_META)],
              meta_v, meta_s, sem)
    write_ids(tbuf, 2, ids_v, meta_v, (4, 4, 2, 3))

    for n, ref in enumerate((m2, p2)):
        for w in range(N // 2):
            rows = slice(w * LANES, (w + 1) * LANES)
            diag = pair_diagonal(ref[ROW_D:ROW_D + TILE, rows])
            flat[n, rows, :] = (DAMPING * dot(diag, ref[rows, :])).astype(BF16)

    def place_row(i, carry):
        rows = pl.ds(pl.multiple_of(i * TILE, TILE), TILE)
        for out in (smm, smp):
            out[rows, :] = jnp.zeros((TILE, WIDE), BF16)
        for w in range(N // 2):
            sides = [halves(flat[n, rows, w * LANES:(w + 1) * LANES]) for n in range(2)]
            for h in range(2):
                for n, out in enumerate((smm, smp)):
                    c = meta_s[n, i, 2 * w + h]
                    out[rows, window(c)] = out[rows, window(c)] + pick(sides[n][h], c)
        return carry

    lax.fori_loop(0, N, place_row, 0)
    for copy in ins:
        copy.wait()
    outs = []
    for n, (ref, sm, j, f, o) in enumerate(((m1, smm, 2, 0, 2), (p1, smp, 0, 3, 4))):
        place_q(qs, ref, TAIL_Q, meta_s, 2 + n)
        pw[...] = (-dot(sm[:, block(j)], qs[...])).astype(BF16)
        cbuf[n] = part[:, block(n)] + dot(ra[:, block(f)], pw[...])
        outs.append(pltpu.make_async_copy(cbuf.at[n], c_ref.at[:, block(o)], out_sem.at[n]))
        outs[n].start()
        write_term(tbuf, n, tpt, cbuf[n], ref, TAIL_T)
    outs.append(pltpu.make_async_copy(tbuf, term_ref.at[:, W:], out_sem.at[2]))
    outs[2].start()
    smm_out[...] = smm[:, 0:2 * W]
    smp_out[...] = smp[:, W:3 * W]
    for out in outs:
        out.wait()


def second(m2, p2, m1, p1, own, m3, p3, part, ra, tpt, c, term):
    shape = jax.ShapeDtypeStruct
    return pl.pallas_call(
        second_kernel,
        out_shape=(
            shape((W, 7 * W), F32), shape((W, 3 * W + LANES), BF16),
            shape((W, 2 * W), BF16), shape((W, 2 * W), BF16),
        ),
        grid=(1,),
        in_specs=[VMEM, VMEM, TAIL, TAIL, TAIL] + [ANY] * 7,
        out_specs=(ANY, ANY, VMEM, VMEM),
        input_output_aliases={10: 0, 11: 1},
        scratch_shapes=[
            pltpu.VMEM((2, W, W), BF16),
            pltpu.VMEM((W, WIDE), BF16),
            pltpu.VMEM((W, WIDE), BF16),
            pltpu.VMEM((W, W), BF16),
            pltpu.VMEM((W, W), BF16),
            pltpu.VMEM((W, 2 * W), F32),
            pltpu.VMEM((W, 4 * W), BF16),
            pltpu.VMEM((W, W), BF16),
            pltpu.VMEM((2, W, W), F32),
            pltpu.VMEM((W, 2 * W + LANES), BF16),
            pltpu.VMEM((5, 16, LANES), I32),
            pltpu.SMEM((5, 16, LANES), I32),
            pltpu.VMEM((CHUNK, LANES), F32),
            pltpu.SemaphoreType.DMA((5,)),
            pltpu.SemaphoreType.DMA((3,)),
            pltpu.SemaphoreType.DMA((3,)),
        ],
        compiler_params=params(),
        cost_estimate=pl.CostEstimate(flops=6_000_000_000, bytes_accessed=12 << 20, transcendentals=0),
    )(m2, p2, m1, p1, own, m3, p3, part, ra, tpt, c, term)


def third_kernel(m3, m2, p2, p3, own, smm, smp, smo, ra, tpt, c_in, c_ref, term,
                 qa, qb, pw, cbuf, meta_v, meta_s, ids_v, sem, out_sem):
    del c_in
    read_meta([(ref, TAIL_META) for ref in (m3, m2, p2, p3, own)], meta_v, meta_s, sem)
    outs = []

    def finish_block(n, value, o, ref):
        cbuf[n] = value
        outs.append(pltpu.make_async_copy(cbuf.at[n], c_ref.at[:, block(o)], out_sem.at[n]))
        outs[-1].start()
        write_term(term, n, tpt, cbuf[n], ref, TAIL_T)

    for two, three, sm, s, mid, far, f1, f2, n2, n3, o2, o3 in (
        (m2, m3, smm, 0, 1, 0, 1, 0, 1, 0, 1, 0),
        (p2, p3, smp, 1, 0, 1, 2, 3, 2, 3, 5, 6),
    ):
        place_q(qa, two, TAIL_Q, meta_s, 1 + s)
        place_q(qb, three, TAIL_Q, meta_s, 3 * s)
        pw[...] = (-dot(smo[:, block(s)], qa[...])).astype(BF16)
        value = dot(ra[:, block(f1)], pw[...])
        pw[...] = (qa[...].astype(F32) - dot(sm[:, block(mid)], qa[...])).astype(BF16)
        finish_block(n2, value + dot(ra[:, block(f2)], pw[...]), o2, two)
        pw[...] = (-dot(sm[:, block(far)], qb[...])).astype(BF16)
        finish_block(n3, dot(ra[:, block(f2)], pw[...]), o3, three)
    write_ids(term, 4, ids_v, meta_v, (4, 0, 1, 2, 3))
    for out in outs:
        out.wait()


def third(m3, m2, p2, p3, own, smm, smp, smo, ra, tpt, c):
    shape = jax.ShapeDtypeStruct
    return pl.pallas_call(
        third_kernel,
        out_shape=(shape((W, 7 * W), F32), shape((W, 4 * W + LANES), BF16)),
        grid=(1,),
        in_specs=[VMEM, TAIL, TAIL, VMEM, TAIL] + [VMEM] * 5 + [ANY],
        out_specs=(ANY, VMEM),
        input_output_aliases={10: 0},
        scratch_shapes=[pltpu.VMEM((W, W), BF16)] * 3
        + [
            pltpu.VMEM((4, W, W), F32),
            pltpu.VMEM((5, 16, LANES), I32),
            pltpu.SMEM((5, 16, LANES), I32),
            pltpu.VMEM((CHUNK, LANES), F32),
            pltpu.SemaphoreType.DMA((5,)),
            pltpu.SemaphoreType.DMA((4,)),
        ],
        compiler_params=params(),
        cost_estimate=pl.CostEstimate(flops=7_000_000_000, bytes_accessed=18 << 20, transcendentals=0),
    )(m3, m2, p2, p3, own, smm, smp, smo, ra, tpt, c)


def gather_pieces(count, x_ref, lows, highs, ids_v, ids_s, sem):
    for p in range(GROUPS):
        ids_v[p] = x_ref[p, 0:8, count * W:].astype(F32).astype(I32)
    to_scalars([(ids_v, ids_s)], sem)
    for y in lows + highs:
        y[...] = jnp.zeros_like(y)

    def one(p, carry):
        rows = pl.ds(pl.multiple_of(p * CHUNK, CHUNK), CHUNK)
        for w in range(N // 2):
            sides = [
                [halves(x_ref[p + d, :, o * W + w * LANES:o * W + (w + 1) * LANES]) for d in (0, GROUPS // 2)]
                for o in range(count)
            ]
            for h in range(2):
                for o in range(count):
                    for y, side, d in ((lows[o], sides[o][0], 0), (highs[o], sides[o][1], GROUPS // 2)):
                        g = ids_s[p + d, 1 + o, 2 * w + h]
                        y[rows, window(g)] = y[rows, window(g)] + pick(side[h], g)
        return carry

    lax.fori_loop(0, GROUPS // 2, one, 0)


def add_pieces(count, first, takes, lows, highs, out_ref):
    for o in range(count):
        total = None
        for cq in range(4):
            cols = slice(cq * QUARTER, (cq + 1) * QUARTER)
            piece = dot(takes[cq, :, 0:256], lows[o][:, cols]) + dot(takes[cq, :, 256:W], highs[o][:, cols])
            total = piece if total is None else total + piece
        out_ref[:, (first + o) * QUARTER:(first + o + 1) * QUARTER] = total.astype(BF16)


def merge_first_kernel(count, x_ref, out_ref, takes, *rest):
    lows, highs, (ids_v, ids_s, sem) = rest[:count], rest[count:2 * count], rest[2 * count:]
    gather_pieces(count, x_ref, lows, highs, ids_v, ids_s, sem)
    groups = jnp.concatenate([ids_v[p, 0:1, :] for p in range(GROUPS)], axis=0).astype(F32).astype(BF16)
    spread = (((iota((LANES, W), 1) >> 2) & 7) == iota((LANES, W), 0)).astype(F32).astype(BF16)
    each = dot(groups, spread)
    mine = (iota((GROUPS, W), 1) >> 5) == iota((GROUPS, W), 0)
    group = jnp.sum(jnp.where(mine, each, 0.0), axis=0, keepdims=True).astype(I32)
    row, col = iota((256, W), 0), iota((256, W), 1)
    hit = ((row >> 4) == group) & ((row & 3) == (col & 3))
    for cq in range(4):
        takes[cq] = (hit & (((row >> 2) & 3) == cq)).astype(F32).astype(BF16)
    add_pieces(count, 0, takes, lows, highs, out_ref)


def merge_last_kernel(count, x_ref, done, takes, out_ref, *rest):
    lows, highs, (ids_v, ids_s, sem) = rest[:count], rest[count:2 * count], rest[2 * count:]
    out_ref[:, 0:done.shape[1]] = done[...]
    gather_pieces(count, x_ref, lows, highs, ids_v, ids_s, sem)
    add_pieces(count, done.shape[1] // QUARTER, takes, lows, highs, out_ref)


def merge(x, done=None, takes=None):
    count = x.shape[2] // W
    shape = jax.ShapeDtypeStruct
    first = done is None
    earlier = 0 if first else done.shape[1] // QUARTER
    out = shape((256, (earlier + count) * QUARTER), BF16)
    return pl.pallas_call(
        functools.partial(merge_first_kernel if first else merge_last_kernel, count),
        out_shape=(out, shape((4, 256, W), BF16)) if first else out,
        in_specs=[VMEM] * (1 if first else 3),
        out_specs=(VMEM, VMEM) if first else VMEM,
        scratch_shapes=[pltpu.VMEM((GROUPS * CHUNK // 2, GROUPS * TILE), BF16)] * (2 * count)
        + [
            pltpu.VMEM((GROUPS, 8, LANES), I32),
            pltpu.SMEM((GROUPS, 8, LANES), I32),
            pltpu.SemaphoreType.DMA((1,)),
        ],
        compiler_params=params(),
        cost_estimate=pl.CostEstimate(flops=1_000_000_000 * count, bytes_accessed=count << 20, transcendentals=0),
    )(*((x,) if first else (x, done, takes)))


def finish_kernel(orders, *refs):
    out_ref = refs[-1]
    row, col = iota((TILE, 256), 0), iota((TILE, 256), 1)
    same = ((row >> 2) == (col >> 4)) & ((row & 3) == (col & 3))
    takes = [(same & (((col >> 2) & 3) == cq)).astype(F32).astype(BF16) for cq in range(4)]
    for order, x_ref in zip(orders, refs):
        for n, o in enumerate(order):
            for cq in range(4):
                at = o * 4 * QUARTER + cq * QUARTER
                out_ref[0, :, at:at + QUARTER] = dot(takes[cq], x_ref[:, n * QUARTER:(n + 1) * QUARTER])


def finish(orders, *parts):
    return pl.pallas_call(
        functools.partial(finish_kernel, orders),
        out_shape=jax.ShapeDtypeStruct((1, TILE, DENSE), F32),
        in_specs=[VMEM] * len(parts),
        out_specs=VMEM,
        compiler_params=params(),
    )(*parts)


def along(block, step):
    count = lax.axis_size("slab")
    route = [(i, i + step) for i in range(count) if 0 <= i + step < count]
    return lax.ppermute(block, "slab", route)


def exchange(term):
    return lax.all_to_all(term.reshape(GROUPS, CHUNK, term.shape[1]), "piece", 0, 0)


def hand_over(dense):
    back = lax.all_to_all(dense.reshape(GROUPS, 16, dense.shape[1]), "piece", 0, 0)
    return back.reshape(256, dense.shape[1])


def per_device(fine_tiles, fine_cols, bond_mask, diag_inv, tentative, aggregate, tentative_two, aggregate_two):
    own = pack(fine_tiles, diag_inv, tentative, tentative_two, fine_cols, bond_mask, aggregate, aggregate_two)
    m1, p1 = along(own, 1), along(own, -1)
    ad, sm, qs, r0, tpt = start_own(own)
    m2, p2 = along(m1, 1), along(p1, -1)
    m3, p3 = along(m1[ROW_Q:], 2), along(p1[ROW_Q:], -2)
    c, term, part, ra, smo = near(m1, p1, ad, sm, qs, r0, tpt, own)
    c, term, smm, smp = second(m2, p2, m1, p1, own, m3, p3, part, ra, tpt, c, term)
    got = exchange(term)
    c, term = third(m3, m2, p2, p3, own, smm, smp, smo, ra, tpt, c)
    last = exchange(term)
    done, takes = merge(got)
    level_two = finish(((3, 2, 4, 0, 1, 5, 6),), hand_over(merge(last, done, takes)))
    return c.reshape(N, TILE, 7 * W), level_two


def solution(mesh):
    both = ("slab", "piece")
    placed = (
        P(both, None, None), P(both, None), P(both, None), P(both, None, None),
        P(both, None, None), P(both), P(both, None, None), P(both),
    )
    return jax.shard_map(
        per_device,
        mesh=mesh,
        in_specs=placed,
        out_specs=(P(both, None, None), P(both, None, None)),
        check_vma=False,
    )
```

```python
import functools

import jax
import jax.numpy as jnp
from jax import lax
from jax.experimental import pallas as pl
from jax.experimental.pallas import tpu as pltpu
from jax.sharding import PartitionSpec as P


DAMPING = 2.0 / 3.0
TILE = 64
N = 8
W = N * TILE
LANES = 128
TRASH = 3 * N
WIDE = 3 * W + LANES
ROW_D, ROW_Q, ROW_T, ROW_META, ROWS = W, W + 64, W + 128, W + 192, W + 208
ANY = pl.BlockSpec(memory_space=pl.ANY)
VMEM = pl.BlockSpec(memory_space=pltpu.VMEM)
BF16, F32, I32 = jnp.bfloat16, jnp.float32, jnp.int32
GROUPS = 16
PART = 4
CHUNK = N * PART
DENSE = 7 * GROUPS * TILE
QUARTER = GROUPS * TILE // 4
TAIL = pl.BlockSpec((144, W), lambda i: (ROW_Q // 144, 0))
TAIL_Q, TAIL_T, TAIL_META = 0, 64, 128


def params():
    return pltpu.CompilerParams(vmem_limit_bytes=62 << 20)


def dot(a, b):
    return jnp.dot(a, b, preferred_element_type=F32)


def iota(shape, dim):
    return lax.broadcasted_iota(I32, shape, dim)


def pack_kernel(a_ref, d_ref, q_ref, t_ref, cols_ref, mask_ref, agg_ref, agg2_ref, out_ref, meta):
    for i in range(N):
        out_ref[i * TILE:(i + 1) * TILE, :] = a_ref[i]
    for row, ref in ((ROW_D, d_ref), (ROW_Q, q_ref), (ROW_T, t_ref)):
        for w in range(N // 2):
            pair = jnp.concatenate([ref[2 * w], ref[2 * w + 1]], axis=1)
            out_ref[row:row + TILE, w * LANES:(w + 1) * LANES] = pair
    meta[...] = jnp.zeros_like(meta)
    meta[0:8, 0:8] = jnp.where(mask_ref[...] > 0, cols_ref[...], TRASH).astype(F32)
    meta[8:9, 0:8] = agg_ref[...].astype(F32)
    meta[9:10, 0:8] = agg2_ref[...].astype(F32)
    out_ref[ROW_META:ROWS, :] = meta[...].astype(BF16)


def pack(a, d, q, t, cols, mask, agg, agg2):
    return pl.pallas_call(
        pack_kernel,
        out_shape=jax.ShapeDtypeStruct((ROWS, W), BF16),
        in_specs=[VMEM] * 8,
        out_specs=VMEM,
        scratch_shapes=[pltpu.VMEM((16, W), F32)],
        compiler_params=params(),
    )(a, d, q, t, cols, mask, agg.reshape(1, N), agg2.reshape(1, N))


def halves(x):
    high = iota(x.shape, 1) >= TILE
    swapped = jnp.concatenate([x[:, TILE:], x[:, :TILE]], axis=1)
    zero = jnp.zeros_like(x)
    return (
        (jnp.where(high, zero, x), jnp.where(high, swapped, zero)),
        (jnp.where(high, zero, swapped), jnp.where(high, x, zero)),
    )


def window(index):
    return pl.ds(pl.multiple_of((index >> 1) * LANES, LANES), LANES)


def pick(variants, index):
    return jnp.where((index & 1) == 1, variants[1], variants[0])


def block_diagonal(row):
    block = iota(row.shape, 1) // TILE
    zero = jnp.zeros_like(row)
    return jnp.concatenate([jnp.where(block == i, row, zero) for i in range(N)], axis=0)


def to_scalars(pairs, sem):
    copies = [pltpu.make_async_copy(v, s, sem.at[n]) for n, (v, s) in enumerate(pairs)]
    for c in copies:
        c.start()
    for c in copies:
        c.wait()


def read_meta(tails, meta_v, meta_s, sem):
    for n, (ref, top) in enumerate(tails):
        meta_v[n] = ref[top:top + 16, 0:LANES].astype(F32).astype(I32)
    to_scalars([(meta_v.at[n], meta_s.at[n]) for n in range(len(tails))], sem)


def place_q(out, ref, top, meta_s, n):
    out[...] = jnp.zeros((W, W), BF16)
    for w in range(N // 2):
        sides = halves(ref[top:top + TILE, w * LANES:(w + 1) * LANES])
        for h in range(2):
            c = 2 * w + h
            g = meta_s[n, 8, c]
            out[c * TILE:(c + 1) * TILE, window(g)] = pick(sides[h], g)


def pair_diagonal(pair):
    high = iota(pair.shape, 1) >= TILE
    zero = jnp.zeros_like(pair)
    return jnp.concatenate([jnp.where(high, zero, pair), jnp.where(high, pair, zero)], axis=0)


def place_a(refs, outs, sms, meta_s, metas):
    def place_row(i, carry):
        rows = pl.ds(pl.multiple_of(i * TILE, TILE), TILE)
        for out in outs:
            out[rows, :] = jnp.zeros((TILE, WIDE), BF16)
        for w in range(N // 2):
            sides = [halves(ref[rows, w * LANES:(w + 1) * LANES]) for ref in refs]
            for h in range(2):
                for out, side, n in zip(outs, sides, metas):
                    c = meta_s[n, i, 2 * w + h]
                    out[rows, window(c)] = out[rows, window(c)] + pick(side[h], c)
        return carry

    lax.fori_loop(0, N, place_row, 0)

    def smooth(w, carry):
        rows = pl.ds(pl.multiple_of(w * LANES, LANES), LANES)
        for ref, out, sm in zip(refs, outs, sms):
            diag = pair_diagonal(ref[ROW_D:ROW_D + TILE, rows])
            sm[rows, :] = (DAMPING * dot(diag, out[rows, 0:3 * W])).astype(BF16)
        return carry

    lax.fori_loop(0, N // 2, smooth, 0)


def write_term(term, n, tpt, c, ref, top):
    lhs = dot(tpt[...], c.astype(BF16)).astype(BF16)
    for w in range(N // 2):
        diag = pair_diagonal(ref[top:top + TILE, w * LANES:(w + 1) * LANES])
        at = n * W + w * LANES
        term[:, at:at + LANES] = dot(lhs[:, w * LANES:(w + 1) * LANES], diag).astype(BF16)


def write_ids(term, count, ids_v, meta_v, order):
    ids_v[...] = jnp.zeros_like(ids_v)
    for row, n in enumerate(order):
        ids_v[row:row + 1, :] = meta_v[n, 9:10, :].astype(F32)
    for q in range(GROUPS):
        term[q * CHUNK:(q + 1) * CHUNK, count * W:] = ids_v[...].astype(BF16)


def block(j):
    return slice(j * W, (j + 1) * W)


def own_kernel(own, rap, sm, qs, r0, tpt, ad, meta_v, meta_s, sem):
    read_meta([(own, ROW_META)], meta_v, meta_s, sem)
    place_q(qs, own, ROW_Q, meta_s, 0)
    place_a((own,), (ad,), (sm,), meta_s, (0,))
    r0[...] = (qs[...].astype(F32) - dot(sm[:, block(1)], qs[...])).astype(BF16)
    turned = r0[...].T
    for j in range(3):
        rap[:, block(j)] = dot(turned, ad[:, block(j)])
    left = block_diagonal(own[ROW_T:ROW_T + TILE, :])
    lead = iota((W, W), 0)
    target = ((lead >> 2) & 7) * TILE + (lead >> 5) * PART + (lead & 3)
    turn = (target == iota((W, W), 1)).astype(F32).astype(BF16)
    tpt[...] = lax.dot_general(turn, left, (((1,), (1,)), ((), ())), preferred_element_type=F32).astype(BF16)


def start_own(own):
    shape = jax.ShapeDtypeStruct
    return pl.pallas_call(
        own_kernel,
        out_shape=(
            shape((W, 3 * W), F32), shape((W, 3 * W), BF16), shape((W, W), BF16),
            shape((W, W), BF16), shape((W, W), BF16),
        ),
        in_specs=[VMEM],
        out_specs=(VMEM,) * 5,
        scratch_shapes=[
            pltpu.VMEM((W, WIDE), BF16),
            pltpu.VMEM((1, 16, LANES), I32),
            pltpu.SMEM((1, 16, LANES), I32),
            pltpu.SemaphoreType.DMA((1,)),
        ],
        compiler_params=params(),
        cost_estimate=pl.CostEstimate(flops=3_000_000_000, bytes_accessed=6 << 20, transcendentals=0),
    )(own)


def fetch(pairs, sem):
    copies = [pltpu.make_async_copy(src, dst, sem.at[n]) for n, (src, dst) in enumerate(pairs)]
    for c in copies:
        c.start()
    return copies


def near_kernel(m1, p1, rap_h, sm_h, qs_h, r0_h, tpt_h, own, c_ref, term_ref, part, ra_out, smo, m1_tail, p1_tail,
                ad0, ad2, sm0, sm1, sm2, qs0, qs1, qs2, rm, r0, rp, tpt, rap, ra, cbuf, tbuf,
                meta_v, meta_s, sem, in_sem, out_sem):
    ins = fetch(((qs_h, qs1), (rap_h, rap), (r0_h, r0), (tpt_h, tpt), (sm_h, sm1)), in_sem)
    m1_tail[...] = m1[ROW_Q:ROWS, :]
    p1_tail[...] = p1[ROW_Q:ROWS, :]
    read_meta([(m1, ROW_META), (p1, ROW_META)], meta_v, meta_s, sem)
    place_a((m1, p1), (ad0, ad2), (sm0, sm2), meta_s, (0, 1))
    for copy in ins:
        copy.wait()

    rm[...] = (-dot(sm0[:, block(2)], qs1[...])).astype(BF16)
    rp[...] = (-dot(sm2[:, block(0)], qs1[...])).astype(BF16)
    before, after = rm[...].T, rp[...].T
    ra[:, block(0)] = dot(before, ad0[:, block(0)]).astype(BF16)
    ra[:, block(1)] = (dot(before, ad0[:, block(1)]) + rap[:, block(0)]).astype(BF16)
    ra[:, block(2)] = (dot(before, ad0[:, block(2)]) + dot(after, ad2[:, block(0)]) + rap[:, block(1)]).astype(BF16)
    ra[:, block(3)] = (dot(after, ad2[:, block(1)]) + rap[:, block(2)]).astype(BF16)
    ra[:, block(4)] = dot(after, ad2[:, block(2)]).astype(BF16)
    for n, f in enumerate((0, 1, 3, 4)):
        ra_out[:, block(n)] = ra[:, block(f)]
    smo[:, block(0)] = sm0[:, block(0)]
    smo[:, block(1)] = sm2[:, block(2)]

    cbuf[...] = dot(ra[:, block(1)], rm[...]) + dot(ra[:, block(2)], r0[...]) + dot(ra[:, block(3)], rp[...])
    out = pltpu.make_async_copy(cbuf, c_ref.at[:, block(3)], out_sem.at[0])
    out.start()
    write_term(tbuf, 0, tpt, cbuf[...], own, TAIL_T)
    sent = pltpu.make_async_copy(tbuf, term_ref.at[:, block(0)], out_sem.at[1])
    sent.start()

    for n, (f, sm, g) in enumerate(((1, sm0, 0), (3, sm2, 2))):
        lead = ra[:, block(f)]
        known = dot(lead, sm[:, block(1)]) + dot(ra[:, block(2)], sm1[:, block(g)])
        part[:, block(n)] = lead.astype(F32) - known
    out.wait()
    sent.wait()


def near(m1, p1, rap, sm, qs, r0, tpt, own):
    shape = jax.ShapeDtypeStruct
    return pl.pallas_call(
        near_kernel,
        grid=(1,),
        out_shape=(
            shape((W, 7 * W), F32), shape((W, 2 * W + LANES), BF16), shape((W, 2 * W), F32),
            shape((W, 4 * W), BF16), shape((W, 2 * W), BF16), shape((144, W), BF16), shape((144, W), BF16),
        ),
        in_specs=[VMEM, VMEM] + [ANY] * 5 + [TAIL],
        out_specs=(ANY, ANY) + (VMEM,) * 5,
        scratch_shapes=[pltpu.VMEM((W, WIDE), BF16)] * 2
        + [pltpu.VMEM((W, 3 * W), BF16)] * 3
        + [pltpu.VMEM((W, W), BF16)] * 7
        + [
            pltpu.VMEM((W, 3 * W), F32),
            pltpu.VMEM((W, 5 * W), BF16),
            pltpu.VMEM((W, W), F32),
            pltpu.VMEM((W, W), BF16),
            pltpu.VMEM((2, 16, LANES), I32),
            pltpu.SMEM((2, 16, LANES), I32),
            pltpu.SemaphoreType.DMA((2,)),
            pltpu.SemaphoreType.DMA((5,)),
            pltpu.SemaphoreType.DMA((2,)),
        ],
        compiler_params=params(),
        cost_estimate=pl.CostEstimate(flops=9_000_000_000, bytes_accessed=14 << 20, transcendentals=0),
    )(m1, p1, rap, sm, qs, r0, tpt, own)


def smooth_far(ref, flat, sm, meta_s, n):
    for w in range(N // 2):
        rows = slice(w * LANES, (w + 1) * LANES)
        diag = pair_diagonal(ref[ROW_D:ROW_D + TILE, rows])
        flat[rows, :] = (DAMPING * dot(diag, ref[rows, :])).astype(BF16)
    tops = (0, W // 2)

    def place_row(i, carry):
        starts = [pl.ds(pl.multiple_of(top + i * TILE, TILE), TILE) for top in tops]
        for rows in starts:
            sm[rows, :] = jnp.zeros((TILE, WIDE), BF16)
        for w in range(N // 2):
            sides = [halves(flat[rows, w * LANES:(w + 1) * LANES]) for rows in starts]
            for h in range(2):
                for d, rows in enumerate(starts):
                    c = meta_s[n, i + d * N // 2, 2 * w + h]
                    sm[rows, window(c)] = sm[rows, window(c)] + pick(sides[d][h], c)
        return carry

    lax.fori_loop(0, N // 2, place_row, 0)


def second_kernel(m2, m1, own, part_h, ra_h, tpt_h, c_in, term_in, c_ref, term_ref, smm_out,
                  flat, smm, qs, pw, part, ra, tpt, cbuf, tbuf, meta_v, meta_s, ids_v, sem, in_sem, out_sem):
    del c_in, term_in
    ins = fetch(((part_h.at[:, block(0)], part), (ra_h.at[:, block(0)], ra), (tpt_h, tpt)), in_sem)
    read_meta([(m2, ROW_META), (m1, TAIL_META), (own, TAIL_META)], meta_v, meta_s, sem)
    write_ids(tbuf, 1, ids_v, meta_v, (2, 2, 1))
    smooth_far(m2, flat, smm, meta_s, 0)
    place_q(qs, m1, TAIL_Q, meta_s, 1)
    for copy in ins:
        copy.wait()
    pw[...] = (part[...] - dot(ra[...], smm[:, block(2)])).astype(BF16)
    cbuf[...] = dot(pw[...], qs[...])
    out = pltpu.make_async_copy(cbuf, c_ref.at[:, block(2)], out_sem.at[0])
    out.start()
    write_term(tbuf, 0, tpt, cbuf[...], m1, TAIL_T)
    sent = pltpu.make_async_copy(tbuf, term_ref.at[:, W:], out_sem.at[1])
    sent.start()
    smm_out[...] = smm[:, 0:2 * W]
    out.wait()
    sent.wait()


def second(m2, m1, own, part, ra, tpt, c, term):
    shape = jax.ShapeDtypeStruct
    return pl.pallas_call(
        second_kernel,
        out_shape=(shape((W, 7 * W), F32), shape((W, 2 * W + LANES), BF16), shape((W, 2 * W), BF16)),
        grid=(1,),
        in_specs=[VMEM, TAIL, TAIL] + [ANY] * 5,
        out_specs=(ANY, ANY, VMEM),
        input_output_aliases={6: 0, 7: 1},
        scratch_shapes=[
            pltpu.VMEM((W, W), BF16),
            pltpu.VMEM((W, WIDE), BF16),
            pltpu.VMEM((W, W), BF16),
            pltpu.VMEM((W, W), BF16),
            pltpu.VMEM((W, W), F32),
            pltpu.VMEM((W, W), BF16),
            pltpu.VMEM((W, W), BF16),
            pltpu.VMEM((W, W), F32),
            pltpu.VMEM((W, W + LANES), BF16),
            pltpu.VMEM((3, 16, LANES), I32),
            pltpu.SMEM((3, 16, LANES), I32),
            pltpu.VMEM((CHUNK, LANES), F32),
            pltpu.SemaphoreType.DMA((3,)),
            pltpu.SemaphoreType.DMA((3,)),
            pltpu.SemaphoreType.DMA((2,)),
        ],
        compiler_params=params(),
        cost_estimate=pl.CostEstimate(flops=4_000_000_000, bytes_accessed=8 << 20, transcendentals=0),
    )(m2, m1, own, part, ra, tpt, c, term)


def third_kernel(p2, p1, m3, m2, p3, own, part, smm, smo, ra, tpt, c_in, c_ref, term,
                 flat, smp, qs, pw, cbuf, meta_v, meta_s, ids_v, sem, out_sem):
    del c_in
    read_meta([(p2, ROW_META)] + [(ref, TAIL_META) for ref in (p1, m2, m3, p3, own)], meta_v, meta_s, sem)
    write_ids(term, 5, ids_v, meta_v, (5, 1, 2, 0, 3, 4))
    smooth_far(p2, flat, smp, meta_s, 0)
    outs = []

    def columns(n, value, o, ref, top, at):
        pw[...] = value.astype(BF16)
        place_q(qs, ref, top, meta_s, at)
        cbuf[n] = dot(pw[...], qs[...])
        outs.append(pltpu.make_async_copy(cbuf.at[n], c_ref.at[:, block(o)], out_sem.at[n]))
        outs[-1].start()
        write_term(term, n, tpt, cbuf[n], ref, top + TILE)

    first, last = ra[:, block(0)], ra[:, block(3)]
    columns(0, part[:, block(1)] - dot(last, smp[:, block(0)]), 4, p1, TAIL_Q, 1)
    value = first.astype(F32) - dot(first, smm[:, block(1)]) - dot(ra[:, block(1)], smo[:, block(0)])
    columns(1, value, 1, m2, TAIL_Q, 2)
    value = last.astype(F32) - dot(last, smp[:, block(1)]) - dot(ra[:, block(2)], smo[:, block(1)])
    columns(2, value, 5, p2, ROW_Q, 0)
    columns(3, -dot(first, smm[:, block(0)]), 0, m3, TAIL_Q, 3)
    columns(4, -dot(last, smp[:, block(2)]), 6, p3, TAIL_Q, 4)
    for out in outs:
        out.wait()


def third(p2, p1, m3, m2, p3, own, part, smm, smo, ra, tpt, c):
    shape = jax.ShapeDtypeStruct
    return pl.pallas_call(
        third_kernel,
        out_shape=(shape((W, 7 * W), F32), shape((W, 5 * W + LANES), BF16)),
        grid=(1,),
        in_specs=[VMEM, TAIL, VMEM, TAIL, VMEM, TAIL] + [VMEM] * 5 + [ANY],
        out_specs=(ANY, VMEM),
        input_output_aliases={11: 0},
        scratch_shapes=[
            pltpu.VMEM((W, W), BF16),
            pltpu.VMEM((W, WIDE), BF16),
            pltpu.VMEM((W, W), BF16),
            pltpu.VMEM((W, W), BF16),
            pltpu.VMEM((5, W, W), F32),
            pltpu.VMEM((6, 16, LANES), I32),
            pltpu.SMEM((6, 16, LANES), I32),
            pltpu.VMEM((CHUNK, LANES), F32),
            pltpu.SemaphoreType.DMA((6,)),
            pltpu.SemaphoreType.DMA((5,)),
        ],
        compiler_params=params(),
        cost_estimate=pl.CostEstimate(flops=7_000_000_000, bytes_accessed=18 << 20, transcendentals=0),
    )(p2, p1, m3, m2, p3, own, part, smm, smo, ra, tpt, c)


def gather_pieces(count, x_ref, lows, highs, ids_v, ids_s, sem):
    for p in range(GROUPS):
        ids_v[p] = x_ref[p, 0:8, count * W:].astype(F32).astype(I32)
    to_scalars([(ids_v, ids_s)], sem)
    for y in lows + highs:
        y[...] = jnp.zeros_like(y)

    def one(p, carry):
        rows = pl.ds(pl.multiple_of(p * CHUNK, CHUNK), CHUNK)
        for w in range(N // 2):
            sides = [
                [halves(x_ref[p + d, :, o * W + w * LANES:o * W + (w + 1) * LANES]) for d in (0, GROUPS // 2)]
                for o in range(count)
            ]
            for h in range(2):
                for o in range(count):
                    for y, side, d in ((lows[o], sides[o][0], 0), (highs[o], sides[o][1], GROUPS // 2)):
                        g = ids_s[p + d, 1 + o, 2 * w + h]
                        y[rows, window(g)] = y[rows, window(g)] + pick(side[h], g)
        return carry

    lax.fori_loop(0, GROUPS // 2, one, 0)


def add_pieces(count, first, takes, lows, highs, out_ref):
    for o in range(count):
        total = None
        for cq in range(4):
            cols = slice(cq * QUARTER, (cq + 1) * QUARTER)
            piece = dot(takes[cq, :, 0:256], lows[o][:, cols]) + dot(takes[cq, :, 256:W], highs[o][:, cols])
            total = piece if total is None else total + piece
        out_ref[:, (first + o) * QUARTER:(first + o + 1) * QUARTER] = total.astype(BF16)


def merge_first_kernel(count, x_ref, out_ref, takes, *rest):
    lows, highs, (ids_v, ids_s, sem) = rest[:count], rest[count:2 * count], rest[2 * count:]
    gather_pieces(count, x_ref, lows, highs, ids_v, ids_s, sem)
    groups = jnp.concatenate([ids_v[p, 0:1, :] for p in range(GROUPS)], axis=0).astype(F32).astype(BF16)
    spread = (((iota((LANES, W), 1) >> 2) & 7) == iota((LANES, W), 0)).astype(F32).astype(BF16)
    each = dot(groups, spread)
    mine = (iota((GROUPS, W), 1) >> 5) == iota((GROUPS, W), 0)
    group = jnp.sum(jnp.where(mine, each, 0.0), axis=0, keepdims=True).astype(I32)
    row, col = iota((256, W), 0), iota((256, W), 1)
    hit = ((row >> 4) == group) & ((row & 3) == (col & 3))
    for cq in range(4):
        takes[cq] = (hit & (((row >> 2) & 3) == cq)).astype(F32).astype(BF16)
    add_pieces(count, 0, takes, lows, highs, out_ref)


def merge_last_kernel(count, x_ref, done, takes, out_ref, *rest):
    lows, highs, (ids_v, ids_s, sem) = rest[:count], rest[count:2 * count], rest[2 * count:]
    out_ref[:, 0:done.shape[1]] = done[...]
    gather_pieces(count, x_ref, lows, highs, ids_v, ids_s, sem)
    add_pieces(count, done.shape[1] // QUARTER, takes, lows, highs, out_ref)


def merge(x, done=None, takes=None):
    count = x.shape[2] // W
    shape = jax.ShapeDtypeStruct
    first = done is None
    earlier = 0 if first else done.shape[1] // QUARTER
    out = shape((256, (earlier + count) * QUARTER), BF16)
    return pl.pallas_call(
        functools.partial(merge_first_kernel if first else merge_last_kernel, count),
        out_shape=(out, shape((4, 256, W), BF16)) if first else out,
        in_specs=[VMEM] * (1 if first else 3),
        out_specs=(VMEM, VMEM) if first else VMEM,
        scratch_shapes=[pltpu.VMEM((GROUPS * CHUNK // 2, GROUPS * TILE), BF16)] * (2 * count)
        + [
            pltpu.VMEM((GROUPS, 8, LANES), I32),
            pltpu.SMEM((GROUPS, 8, LANES), I32),
            pltpu.SemaphoreType.DMA((1,)),
        ],
        compiler_params=params(),
        cost_estimate=pl.CostEstimate(flops=1_000_000_000 * count, bytes_accessed=count << 20, transcendentals=0),
    )(*((x,) if first else (x, done, takes)))


def finish_kernel(orders, *refs):
    out_ref = refs[-1]
    row, col = iota((TILE, 256), 0), iota((TILE, 256), 1)
    same = ((row >> 2) == (col >> 4)) & ((row & 3) == (col & 3))
    takes = [(same & (((col >> 2) & 3) == cq)).astype(F32).astype(BF16) for cq in range(4)]
    for order, x_ref in zip(orders, refs):
        for n, o in enumerate(order):
            for cq in range(4):
                at = o * 4 * QUARTER + cq * QUARTER
                out_ref[0, :, at:at + QUARTER] = dot(takes[cq], x_ref[:, n * QUARTER:(n + 1) * QUARTER])


def finish(orders, *parts):
    return pl.pallas_call(
        functools.partial(finish_kernel, orders),
        out_shape=jax.ShapeDtypeStruct((1, TILE, DENSE), F32),
        in_specs=[VMEM] * len(parts),
        out_specs=VMEM,
        compiler_params=params(),
    )(*parts)


def along(block, step):
    count = lax.axis_size("slab")
    route = [(i, i + step) for i in range(count) if 0 <= i + step < count]
    return lax.ppermute(block, "slab", route)


def exchange(term):
    return lax.all_to_all(term.reshape(GROUPS, CHUNK, term.shape[1]), "piece", 0, 0)


def hand_over(dense):
    back = lax.all_to_all(dense.reshape(GROUPS, 16, dense.shape[1]), "piece", 0, 0)
    return back.reshape(256, dense.shape[1])


def device_part(fine_tiles, fine_cols, bond_mask, diag_inv, tentative, aggregate, tentative_two, aggregate_two):
    own = pack(fine_tiles, diag_inv, tentative, tentative_two, fine_cols, bond_mask, aggregate, aggregate_two)
    m1, p1 = along(own, 1), along(own, -1)
    rap, sm, qs, r0, tpt = start_own(own)
    m2 = along(m1, 1)
    p2 = along(p1, -1)
    c, term, part, ra, smo, m1_tail, p1_tail = near(m1, p1, rap, sm, qs, r0, tpt, own)
    m3 = along(m1_tail, 2)
    p3 = along(p1_tail, -2)
    c, term, smm = second(m2, m1, own, part, ra, tpt, c, term)
    got = exchange(term)
    c, term = third(p2, p1, m3, m2, p3, own, part, smm, smo, ra, tpt, c)
    last = exchange(term)
    done, takes = merge(got)
    level_two = finish(((3, 2, 4, 1, 5, 0, 6),), hand_over(merge(last, done, takes)))
    return c.reshape(N, TILE, 7 * W), level_two


def solution(mesh):
    both = ("slab", "piece")
    placed = (
        P(both, None, None), P(both, None), P(both, None), P(both, None, None),
        P(both, None, None), P(both), P(both, None, None), P(both),
    )
    return jax.shard_map(
        device_part,
        mesh=mesh,
        in_specs=placed,
        out_specs=(P(both, None, None), P(both, None, None)),
        check_vma=False,
    )
```

```python
import functools

import jax
import jax.numpy as jnp
from jax import lax
from jax.experimental import pallas as pl
from jax.experimental.pallas import tpu as pltpu
from jax.sharding import PartitionSpec as P


DAMPING = 2.0 / 3.0
TILE = 64
N = 8
W = N * TILE
LANES = 128
TRASH = 3 * N
WIDE = 3 * W + LANES
ROW_D, ROW_Q, ROW_T, ROW_META, ROWS = W, W + 64, W + 128, W + 192, W + 208
ANY = pl.BlockSpec(memory_space=pl.ANY)
VMEM = pl.BlockSpec(memory_space=pltpu.VMEM)
SMEM = pl.BlockSpec(memory_space=pltpu.SMEM)
BF16, F32, I32 = jnp.bfloat16, jnp.float32, jnp.int32
GROUPS = 16
PART = 4
CHUNK = N * PART
DENSE = 7 * GROUPS * TILE
QUARTER = GROUPS * TILE // 4
TAIL = pl.BlockSpec((144, W), lambda i: (ROW_Q // 144, 0))
TAIL_Q, TAIL_T, TAIL_META = 0, 64, 128


def params():
    return pltpu.CompilerParams(vmem_limit_bytes=62 << 20)


def dot(a, b):
    return jnp.dot(a, b, preferred_element_type=F32)


def iota(shape, dim):
    return lax.broadcasted_iota(I32, shape, dim)


def pack_kernel(a_ref, d_ref, q_ref, t_ref, cols_ref, mask_ref, agg_ref, agg2_ref, out_ref, meta):
    for i in range(N):
        out_ref[i * TILE:(i + 1) * TILE, :] = a_ref[i]
    for row, ref in ((ROW_D, d_ref), (ROW_Q, q_ref), (ROW_T, t_ref)):
        for w in range(N // 2):
            pair = jnp.concatenate([ref[2 * w], ref[2 * w + 1]], axis=1)
            out_ref[row:row + TILE, w * LANES:(w + 1) * LANES] = pair
    meta[...] = jnp.zeros_like(meta)
    meta[0:8, 0:8] = jnp.where(mask_ref[...] > 0, cols_ref[...], TRASH).astype(F32)
    meta[8:9, 0:8] = agg_ref[...].astype(F32)
    meta[9:10, 0:8] = agg2_ref[...].astype(F32)
    out_ref[ROW_META:ROWS, :] = meta[...].astype(BF16)


def pack(a, d, q, t, cols, mask, agg, agg2):
    return pl.pallas_call(
        pack_kernel,
        out_shape=jax.ShapeDtypeStruct((ROWS, W), BF16),
        in_specs=[VMEM] * 8,
        out_specs=VMEM,
        scratch_shapes=[pltpu.VMEM((16, W), F32)],
        compiler_params=params(),
    )(a, d, q, t, cols, mask, agg.reshape(1, N), agg2.reshape(1, N))


def halves(x):
    high = iota(x.shape, 1) >= TILE
    swapped = jnp.concatenate([x[:, TILE:], x[:, :TILE]], axis=1)
    zero = jnp.zeros_like(x)
    return (
        (jnp.where(high, zero, x), jnp.where(high, swapped, zero)),
        (jnp.where(high, zero, swapped), jnp.where(high, x, zero)),
    )


def window(index):
    return pl.ds(pl.multiple_of((index >> 1) * LANES, LANES), LANES)


def pick(variants, index):
    return jnp.where((index & 1) == 1, variants[1], variants[0])


def block_diagonal(row):
    block = iota(row.shape, 1) // TILE
    zero = jnp.zeros_like(row)
    return jnp.concatenate([jnp.where(block == i, row, zero) for i in range(N)], axis=0)


def to_scalars(pairs, sem):
    copies = [pltpu.make_async_copy(v, s, sem.at[n]) for n, (v, s) in enumerate(pairs)]
    for c in copies:
        c.start()
    for c in copies:
        c.wait()


def read_meta(tails, meta_v, meta_s, sem):
    for n, (ref, top) in enumerate(tails):
        meta_v[n] = ref[top:top + 16, 0:LANES].astype(F32).astype(I32)
    to_scalars([(meta_v.at[n], meta_s.at[n]) for n in range(len(tails))], sem)


def inside(slab, step, slabs):
    at = slab[0] + step
    return (at >= 0) & (at < slabs)


def place_q(out, ref, top, meta_s, n, valid=None):
    out[...] = jnp.zeros((W, W), BF16)
    for w in range(N // 2):
        sides = halves(ref[top:top + TILE, w * LANES:(w + 1) * LANES])
        for h in range(2):
            c = 2 * w + h
            g = meta_s[n, 8, c]
            out[c * TILE:(c + 1) * TILE, window(g)] = pick(sides[h], g)
    if valid is not None:
        @pl.when(jnp.logical_not(valid))
        def _():
            out[...] = jnp.zeros((W, W), BF16)


def pair_diagonal(pair):
    high = iota(pair.shape, 1) >= TILE
    zero = jnp.zeros_like(pair)
    return jnp.concatenate([jnp.where(high, zero, pair), jnp.where(high, pair, zero)], axis=0)


def place_a(refs, outs, sms, meta_s, metas, valids=None):
    def place_row(i, carry):
        rows = pl.ds(pl.multiple_of(i * TILE, TILE), TILE)
        for out in outs:
            out[rows, :] = jnp.zeros((TILE, WIDE), BF16)
        for w in range(N // 2):
            sides = [halves(ref[rows, w * LANES:(w + 1) * LANES]) for ref in refs]
            for h in range(2):
                for out, side, n in zip(outs, sides, metas):
                    c = meta_s[n, i, 2 * w + h]
                    if valids is not None:
                        c = jnp.where(valids[n], c, TRASH)
                    out[rows, window(c)] = out[rows, window(c)] + pick(side[h], c)
        return carry

    lax.fori_loop(0, N, place_row, 0)

    def smooth(w, carry):
        rows = pl.ds(pl.multiple_of(w * LANES, LANES), LANES)
        for ref, out, sm in zip(refs, outs, sms):
            diag = pair_diagonal(ref[ROW_D:ROW_D + TILE, rows])
            sm[rows, :] = (DAMPING * dot(diag, out[rows, 0:3 * W])).astype(BF16)
        return carry

    lax.fori_loop(0, N // 2, smooth, 0)


def write_term(term, n, tpt, c, ref, top):
    lhs = dot(tpt[...], c.astype(BF16)).astype(BF16)
    for w in range(N // 2):
        diag = pair_diagonal(ref[top:top + TILE, w * LANES:(w + 1) * LANES])
        at = n * W + w * LANES
        term[:, at:at + LANES] = dot(lhs[:, w * LANES:(w + 1) * LANES], diag).astype(BF16)


def write_ids(term, count, ids_v, meta_v, order):
    ids_v[...] = jnp.zeros_like(ids_v)
    for row, n in enumerate(order):
        ids_v[row:row + 1, :] = meta_v[n, 9:10, :].astype(F32)
    for q in range(GROUPS):
        term[q * CHUNK:(q + 1) * CHUNK, count * W:] = ids_v[...].astype(BF16)


def block(j):
    return slice(j * W, (j + 1) * W)


def own_kernel(own, rap, sm, qs, r0, tpt, ad, meta_v, meta_s, sem):
    read_meta([(own, ROW_META)], meta_v, meta_s, sem)
    place_q(qs, own, ROW_Q, meta_s, 0)
    place_a((own,), (ad,), (sm,), meta_s, (0,))
    r0[...] = (qs[...].astype(F32) - dot(sm[:, block(1)], qs[...])).astype(BF16)
    turned = r0[...].T
    for j in range(3):
        rap[:, block(j)] = dot(turned, ad[:, block(j)])
    left = block_diagonal(own[ROW_T:ROW_T + TILE, :])
    lead = iota((W, W), 0)
    target = ((lead >> 2) & 7) * TILE + (lead >> 5) * PART + (lead & 3)
    turn = (target == iota((W, W), 1)).astype(F32).astype(BF16)
    tpt[...] = lax.dot_general(turn, left, (((1,), (1,)), ((), ())), preferred_element_type=F32).astype(BF16)


def start_own(own):
    shape = jax.ShapeDtypeStruct
    return pl.pallas_call(
        own_kernel,
        out_shape=(
            shape((W, 3 * W), F32), shape((W, 3 * W), BF16), shape((W, W), BF16),
            shape((W, W), BF16), shape((W, W), BF16),
        ),
        in_specs=[VMEM],
        out_specs=(VMEM,) * 5,
        scratch_shapes=[
            pltpu.VMEM((W, WIDE), BF16),
            pltpu.VMEM((1, 16, LANES), I32),
            pltpu.SMEM((1, 16, LANES), I32),
            pltpu.SemaphoreType.DMA((1,)),
        ],
        compiler_params=params(),
        cost_estimate=pl.CostEstimate(flops=3_000_000_000, bytes_accessed=6 << 20, transcendentals=0),
    )(own)


def fetch(pairs, sem):
    copies = [pltpu.make_async_copy(src, dst, sem.at[n]) for n, (src, dst) in enumerate(pairs)]
    for c in copies:
        c.start()
    return copies


def near_kernel(slabs, slab, m1, p1, rap_h, sm_h, qs_h, r0_h, tpt_h, own,
                c_ref, term_ref, part_h, ra_h, smo_h, m1_tail, p1_tail,
                ad0, ad2, sm0, sm1, sm2, qs1, rm, r0, rp, tpt, rap, ra, part, cbuf, tbuf,
                meta_v, meta_s, sem, in_sem, out_sem):
    ins = fetch(((qs_h, qs1), (rap_h, rap), (r0_h, r0), (tpt_h, tpt), (sm_h, sm1)), in_sem)
    outs = []

    def send(src, dst):
        outs.append(pltpu.make_async_copy(src, dst, out_sem.at[len(outs)]))
        outs[-1].start()

    send(m1.at[ROW_Q:ROWS, :], m1_tail)
    send(p1.at[ROW_Q:ROWS, :], p1_tail)
    read_meta([(m1, ROW_META), (p1, ROW_META)], meta_v, meta_s, sem)
    valids = (inside(slab, -1, slabs), inside(slab, 1, slabs))
    place_a((m1, p1), (ad0, ad2), (sm0, sm2), meta_s, (0, 1), valids)
    send(sm0.at[:, block(0)], smo_h.at[:, block(0)])
    send(sm2.at[:, W:3 * W], smo_h.at[:, W:3 * W])
    for copy in ins:
        copy.wait()

    rm[...] = (-dot(sm0[:, block(2)], qs1[...])).astype(BF16)
    rp[...] = (-dot(sm2[:, block(0)], qs1[...])).astype(BF16)
    before, after = rm[...].T, rp[...].T
    ra[:, block(0)] = dot(before, ad0[:, block(0)]).astype(BF16)
    ra[:, block(1)] = (dot(before, ad0[:, block(1)]) + rap[:, block(0)]).astype(BF16)
    ra[:, block(2)] = (dot(before, ad0[:, block(2)]) + dot(after, ad2[:, block(0)]) + rap[:, block(1)]).astype(BF16)
    ra[:, block(3)] = (dot(after, ad2[:, block(1)]) + rap[:, block(2)]).astype(BF16)
    ra[:, block(4)] = dot(after, ad2[:, block(2)]).astype(BF16)
    send(ra, ra_h)

    lead = ra[:, block(1)]
    part[...] = lead.astype(F32) - dot(lead, sm0[:, block(1)]) - dot(ra[:, block(2)], sm1[:, block(0)])
    send(part, part_h)
    cbuf[...] = dot(ra[:, block(1)], rm[...]) + dot(ra[:, block(2)], r0[...]) + dot(ra[:, block(3)], rp[...])
    send(cbuf, c_ref.at[:, block(3)])
    write_term(tbuf, 0, tpt, cbuf[...], own, TAIL_T)
    send(tbuf, term_ref.at[:, block(0)])
    for copy in outs:
        copy.wait()


def near(slab, m1, p1, rap, sm, qs, r0, tpt, own):
    shape = jax.ShapeDtypeStruct
    return pl.pallas_call(
        functools.partial(near_kernel, lax.axis_size("slab")),
        grid=(1,),
        out_shape=(
            shape((W, 7 * W), F32), shape((W, 2 * W + LANES), BF16), shape((W, W), F32),
            shape((W, 5 * W), BF16), shape((W, 3 * W), BF16), shape((144, W), BF16), shape((144, W), BF16),
        ),
        in_specs=[SMEM, VMEM, VMEM] + [ANY] * 5 + [TAIL],
        out_specs=(ANY,) * 7,
        scratch_shapes=[pltpu.VMEM((W, WIDE), BF16)] * 2
        + [pltpu.VMEM((W, 3 * W), BF16)] * 3
        + [pltpu.VMEM((W, W), BF16)] * 5
        + [
            pltpu.VMEM((W, 3 * W), F32),
            pltpu.VMEM((W, 5 * W), BF16),
            pltpu.VMEM((W, W), F32),
            pltpu.VMEM((W, W), F32),
            pltpu.VMEM((W, W), BF16),
            pltpu.VMEM((2, 16, LANES), I32),
            pltpu.SMEM((2, 16, LANES), I32),
            pltpu.SemaphoreType.DMA((2,)),
            pltpu.SemaphoreType.DMA((5,)),
            pltpu.SemaphoreType.DMA((8,)),
        ],
        compiler_params=params(),
        cost_estimate=pl.CostEstimate(flops=9_000_000_000, bytes_accessed=14 << 20, transcendentals=0),
    )(slab, m1, p1, rap, sm, qs, r0, tpt, own)


def smooth_far(ref, flat, sm, meta_s, n, valid):
    for w in range(N // 2):
        rows = slice(w * LANES, (w + 1) * LANES)
        diag = pair_diagonal(ref[ROW_D:ROW_D + TILE, rows])
        flat[rows, :] = (DAMPING * dot(diag, ref[rows, :])).astype(BF16)
    tops = (0, W // 2)

    def place_row(i, carry):
        starts = [pl.ds(pl.multiple_of(top + i * TILE, TILE), TILE) for top in tops]
        for rows in starts:
            sm[rows, :] = jnp.zeros((TILE, WIDE), BF16)
        for w in range(N // 2):
            sides = [halves(flat[rows, w * LANES:(w + 1) * LANES]) for rows in starts]
            for h in range(2):
                for d, rows in enumerate(starts):
                    c = jnp.where(valid, meta_s[n, i + d * N // 2, 2 * w + h], TRASH)
                    sm[rows, window(c)] = sm[rows, window(c)] + pick(sides[d][h], c)
        return carry

    lax.fori_loop(0, N // 2, place_row, 0)


def second_kernel(slabs, slab, m2, m1, own, part_h, ra_h, tpt_h, c_in, term_in, c_ref, term_ref, smm_out,
                  flat, smm, qs, pw, part, ra, tpt, cbuf, tbuf, meta_v, meta_s, ids_v, sem, in_sem, out_sem):
    del c_in, term_in
    ins = fetch(((part_h, part), (ra_h.at[:, block(0)], ra), (tpt_h, tpt)), in_sem)
    read_meta([(m2, ROW_META), (m1, TAIL_META), (own, TAIL_META)], meta_v, meta_s, sem)
    write_ids(tbuf, 1, ids_v, meta_v, (2, 2, 1))
    smooth_far(m2, flat, smm, meta_s, 0, inside(slab, -2, slabs))
    place_q(qs, m1, TAIL_Q, meta_s, 1, inside(slab, -1, slabs))
    for copy in ins:
        copy.wait()
    pw[...] = (part[...] - dot(ra[...], smm[:, block(2)])).astype(BF16)
    cbuf[...] = dot(pw[...], qs[...])
    out = pltpu.make_async_copy(cbuf, c_ref.at[:, block(2)], out_sem.at[0])
    out.start()
    write_term(tbuf, 0, tpt, cbuf[...], m1, TAIL_T)
    sent = pltpu.make_async_copy(tbuf, term_ref.at[:, W:], out_sem.at[1])
    sent.start()
    smm_out[...] = smm[:, 0:2 * W]
    out.wait()
    sent.wait()


def second(slab, m2, m1, own, part, ra, tpt, c, term):
    shape = jax.ShapeDtypeStruct
    return pl.pallas_call(
        functools.partial(second_kernel, lax.axis_size("slab")),
        out_shape=(shape((W, 7 * W), F32), shape((W, 2 * W + LANES), BF16), shape((W, 2 * W), BF16)),
        grid=(1,),
        in_specs=[SMEM, VMEM, TAIL, TAIL] + [ANY] * 5,
        out_specs=(ANY, ANY, VMEM),
        input_output_aliases={7: 0, 8: 1},
        scratch_shapes=[
            pltpu.VMEM((W, W), BF16),
            pltpu.VMEM((W, WIDE), BF16),
            pltpu.VMEM((W, W), BF16),
            pltpu.VMEM((W, W), BF16),
            pltpu.VMEM((W, W), F32),
            pltpu.VMEM((W, W), BF16),
            pltpu.VMEM((W, W), BF16),
            pltpu.VMEM((W, W), F32),
            pltpu.VMEM((W, W + LANES), BF16),
            pltpu.VMEM((3, 16, LANES), I32),
            pltpu.SMEM((3, 16, LANES), I32),
            pltpu.VMEM((CHUNK, LANES), F32),
            pltpu.SemaphoreType.DMA((3,)),
            pltpu.SemaphoreType.DMA((3,)),
            pltpu.SemaphoreType.DMA((2,)),
        ],
        compiler_params=params(),
        cost_estimate=pl.CostEstimate(flops=4_000_000_000, bytes_accessed=8 << 20, transcendentals=0),
    )(slab, m2, m1, own, part, ra, tpt, c, term)


def third_kernel(slabs, slab, p2, p1, m3, m2, p3, own, sm_h, smm_h, smo_h, ra_h, tpt_h, c_in, c_ref, term,
                 flat, smp, qs, pw, cbuf, sm1, smm, smo, ra, tpt, meta_v, meta_s, ids_v, sem, in_sem, out_sem):
    del c_in
    ins = fetch(((sm_h.at[:, block(2)], sm1), (smm_h, smm), (smo_h, smo), (ra_h, ra), (tpt_h, tpt)), in_sem)
    read_meta([(p2, ROW_META)] + [(ref, TAIL_META) for ref in (p1, m2, m3, p3, own)], meta_v, meta_s, sem)
    write_ids(term, 5, ids_v, meta_v, (5, 1, 2, 0, 3, 4))
    smooth_far(p2, flat, smp, meta_s, 0, inside(slab, 2, slabs))
    for copy in ins:
        copy.wait()
    outs = []

    def columns(n, value, o, ref, top, at):
        pw[...] = value.astype(BF16)
        place_q(qs, ref, top, meta_s, at, inside(slab, o - 3, slabs))
        cbuf[n] = dot(pw[...], qs[...])
        outs.append(pltpu.make_async_copy(cbuf.at[n], c_ref.at[:, block(o)], out_sem.at[n]))
        outs[-1].start()
        write_term(term, n, tpt, cbuf[n], ref, top + TILE)

    first, last = ra[:, block(0)], ra[:, block(4)]
    near = ra[:, block(3)]
    value = near.astype(F32) - dot(near, smo[:, block(1)]) - dot(ra[:, block(2)], sm1[...])
    columns(0, value - dot(last, smp[:, block(0)]), 4, p1, TAIL_Q, 1)
    value = first.astype(F32) - dot(first, smm[:, block(1)]) - dot(ra[:, block(1)], smo[:, block(0)])
    columns(1, value, 1, m2, TAIL_Q, 2)
    value = last.astype(F32) - dot(last, smp[:, block(1)]) - dot(near, smo[:, block(2)])
    columns(2, value, 5, p2, ROW_Q, 0)
    columns(3, -dot(first, smm[:, block(0)]), 0, m3, TAIL_Q, 3)
    columns(4, -dot(last, smp[:, block(2)]), 6, p3, TAIL_Q, 4)
    for out in outs:
        out.wait()


def third(slab, p2, p1, m3, m2, p3, own, sm, smm, smo, ra, tpt, c):
    shape = jax.ShapeDtypeStruct
    return pl.pallas_call(
        functools.partial(third_kernel, lax.axis_size("slab")),
        out_shape=(shape((W, 7 * W), F32), shape((W, 5 * W + LANES), BF16)),
        grid=(1,),
        in_specs=[SMEM, VMEM, TAIL, VMEM, TAIL, VMEM, TAIL] + [ANY] * 6,
        out_specs=(ANY, VMEM),
        input_output_aliases={12: 0},
        scratch_shapes=[
            pltpu.VMEM((W, W), BF16),
            pltpu.VMEM((W, WIDE), BF16),
            pltpu.VMEM((W, W), BF16),
            pltpu.VMEM((W, W), BF16),
            pltpu.VMEM((5, W, W), F32),
            pltpu.VMEM((W, W), BF16),
            pltpu.VMEM((W, 2 * W), BF16),
            pltpu.VMEM((W, 3 * W), BF16),
            pltpu.VMEM((W, 5 * W), BF16),
            pltpu.VMEM((W, W), BF16),
            pltpu.VMEM((6, 16, LANES), I32),
            pltpu.SMEM((6, 16, LANES), I32),
            pltpu.VMEM((CHUNK, LANES), F32),
            pltpu.SemaphoreType.DMA((6,)),
            pltpu.SemaphoreType.DMA((5,)),
            pltpu.SemaphoreType.DMA((5,)),
        ],
        compiler_params=params(),
        cost_estimate=pl.CostEstimate(flops=7_000_000_000, bytes_accessed=18 << 20, transcendentals=0),
    )(slab, p2, p1, m3, m2, p3, own, sm, smm, smo, ra, tpt, c)


def gather_pieces(count, x_ref, lows, highs, ids_v, ids_s, sem):
    for p in range(GROUPS):
        ids_v[p] = x_ref[p, 0:8, count * W:].astype(F32).astype(I32)
    to_scalars([(ids_v, ids_s)], sem)
    for y in lows + highs:
        y[...] = jnp.zeros_like(y)

    def one(p, carry):
        rows = pl.ds(pl.multiple_of(p * CHUNK, CHUNK), CHUNK)
        for w in range(N // 2):
            sides = [
                [halves(x_ref[p + d, :, o * W + w * LANES:o * W + (w + 1) * LANES]) for d in (0, GROUPS // 2)]
                for o in range(count)
            ]
            for h in range(2):
                for o in range(count):
                    for y, side, d in ((lows[o], sides[o][0], 0), (highs[o], sides[o][1], GROUPS // 2)):
                        g = ids_s[p + d, 1 + o, 2 * w + h]
                        y[rows, window(g)] = y[rows, window(g)] + pick(side[h], g)
        return carry

    lax.fori_loop(0, GROUPS // 2, one, 0)


def add_pieces(count, first, takes, lows, highs, out_ref):
    for o in range(count):
        total = None
        for cq in range(4):
            cols = slice(cq * QUARTER, (cq + 1) * QUARTER)
            piece = dot(takes[cq, :, 0:256], lows[o][:, cols]) + dot(takes[cq, :, 256:W], highs[o][:, cols])
            total = piece if total is None else total + piece
        out_ref[:, (first + o) * QUARTER:(first + o + 1) * QUARTER] = total.astype(BF16)


def merge_first_kernel(count, x_ref, out_ref, takes, *rest):
    lows, highs, (ids_v, ids_s, sem) = rest[:count], rest[count:2 * count], rest[2 * count:]
    gather_pieces(count, x_ref, lows, highs, ids_v, ids_s, sem)
    groups = jnp.concatenate([ids_v[p, 0:1, :] for p in range(GROUPS)], axis=0).astype(F32).astype(BF16)
    spread = (((iota((LANES, W), 1) >> 2) & 7) == iota((LANES, W), 0)).astype(F32).astype(BF16)
    each = dot(groups, spread)
    mine = (iota((GROUPS, W), 1) >> 5) == iota((GROUPS, W), 0)
    group = jnp.sum(jnp.where(mine, each, 0.0), axis=0, keepdims=True).astype(I32)
    row, col = iota((256, W), 0), iota((256, W), 1)
    hit = ((row >> 4) == group) & ((row & 3) == (col & 3))
    for cq in range(4):
        takes[cq] = (hit & (((row >> 2) & 3) == cq)).astype(F32).astype(BF16)
    add_pieces(count, 0, takes, lows, highs, out_ref)


def merge_last_kernel(count, x_ref, done, takes, out_ref, *rest):
    lows, highs, (ids_v, ids_s, sem) = rest[:count], rest[count:2 * count], rest[2 * count:]
    out_ref[:, 0:done.shape[1]] = done[...]
    gather_pieces(count, x_ref, lows, highs, ids_v, ids_s, sem)
    add_pieces(count, done.shape[1] // QUARTER, takes, lows, highs, out_ref)


def merge(x, done=None, takes=None):
    count = x.shape[2] // W
    shape = jax.ShapeDtypeStruct
    first = done is None
    earlier = 0 if first else done.shape[1] // QUARTER
    out = shape((256, (earlier + count) * QUARTER), BF16)
    return pl.pallas_call(
        functools.partial(merge_first_kernel if first else merge_last_kernel, count),
        out_shape=(out, shape((4, 256, W), BF16)) if first else out,
        in_specs=[VMEM] * (1 if first else 3),
        out_specs=(VMEM, VMEM) if first else VMEM,
        scratch_shapes=[pltpu.VMEM((GROUPS * CHUNK // 2, GROUPS * TILE), BF16)] * (2 * count)
        + [
            pltpu.VMEM((GROUPS, 8, LANES), I32),
            pltpu.SMEM((GROUPS, 8, LANES), I32),
            pltpu.SemaphoreType.DMA((1,)),
        ],
        compiler_params=params(),
        cost_estimate=pl.CostEstimate(flops=1_000_000_000 * count, bytes_accessed=count << 20, transcendentals=0),
    )(*((x,) if first else (x, done, takes)))


def finish_kernel(orders, *refs):
    out_ref = refs[-1]
    row, col = iota((TILE, 256), 0), iota((TILE, 256), 1)
    same = ((row >> 2) == (col >> 4)) & ((row & 3) == (col & 3))
    takes = [(same & (((col >> 2) & 3) == cq)).astype(F32).astype(BF16) for cq in range(4)]
    for order, x_ref in zip(orders, refs):
        for n, o in enumerate(order):
            for cq in range(4):
                at = o * 4 * QUARTER + cq * QUARTER
                out_ref[0, :, at:at + QUARTER] = dot(takes[cq], x_ref[:, n * QUARTER:(n + 1) * QUARTER])


def finish(orders, *parts):
    return pl.pallas_call(
        functools.partial(finish_kernel, orders),
        out_shape=jax.ShapeDtypeStruct((1, TILE, DENSE), F32),
        in_specs=[VMEM] * len(parts),
        out_specs=VMEM,
        compiler_params=params(),
    )(*parts)


def along(block, step):
    count = lax.axis_size("slab")
    route = [(i, (i + step) % count) for i in range(count)]
    return lax.ppermute(block, "slab", route)


def exchange(term):
    return lax.all_to_all(term.reshape(GROUPS, CHUNK, term.shape[1]), "piece", 0, 0)


def hand_over(dense):
    back = lax.all_to_all(dense.reshape(GROUPS, 16, dense.shape[1]), "piece", 0, 0)
    return back.reshape(256, dense.shape[1])


def device_part(fine_tiles, fine_cols, bond_mask, diag_inv, tentative, aggregate, tentative_two, aggregate_two):
    own = pack(fine_tiles, diag_inv, tentative, tentative_two, fine_cols, bond_mask, aggregate, aggregate_two)
    m1, p1 = along(own, 1), along(own, -1)
    slab = lax.axis_index("slab").astype(I32).reshape(1)
    rap, sm, qs, r0, tpt = start_own(own)
    m2 = along(m1, 1)
    p2 = along(p1, -1)
    c, term, part, ra, smo, m1_tail, p1_tail = near(slab, m1, p1, rap, sm, qs, r0, tpt, own)
    m3 = along(m1_tail, 2)
    p3 = along(p1_tail, -2)
    c, term, smm = second(slab, m2, m1, own, part, ra, tpt, c, term)
    got = exchange(term)
    c, term = third(slab, p2, p1, m3, m2, p3, own, sm, smm, smo, ra, tpt, c)
    last = exchange(term)
    done, takes = merge(got)
    level_two = finish(((3, 2, 4, 1, 5, 0, 6),), hand_over(merge(last, done, takes)))
    return c.reshape(N, TILE, 7 * W), level_two


def solution(mesh):
    both = ("slab", "piece")
    placed = (
        P(both, None, None), P(both, None), P(both, None), P(both, None, None),
        P(both, None, None), P(both), P(both, None, None), P(both),
    )
    return jax.shard_map(
        device_part,
        mesh=mesh,
        in_specs=placed,
        out_specs=(P(both, None, None), P(both, None, None)),
        check_vma=False,
    )
```

```python
import functools

import jax
import jax.numpy as jnp
from jax import lax
from jax.experimental import pallas as pl
from jax.experimental.pallas import tpu as pltpu
from jax.sharding import PartitionSpec as P


DAMPING = 2.0 / 3.0
TILE = 64
N = 8
W = N * TILE
LANES = 128
TRASH = 3 * N
WIDE = 3 * W + LANES
ROW_D, ROW_Q, ROW_T, ROW_META, ROWS = W, W + 64, W + 128, W + 192, W + 208
ANY = pl.BlockSpec(memory_space=pl.ANY)
VMEM = pl.BlockSpec(memory_space=pltpu.VMEM)
SMEM = pl.BlockSpec(memory_space=pltpu.SMEM)
BF16, F32, I32 = jnp.bfloat16, jnp.float32, jnp.int32
GROUPS = 16
PART = 4
CHUNK = N * PART
DENSE = 7 * GROUPS * TILE
QUARTER = GROUPS * TILE // 4
TAIL = pl.BlockSpec((144, W), lambda i: (ROW_Q // 144, 0))
TAIL_Q, TAIL_T, TAIL_META = 0, 64, 128


def params():
    return pltpu.CompilerParams(vmem_limit_bytes=67_043_328)


def dot(a, b):
    return jnp.dot(a, b, preferred_element_type=F32)


def iota(shape, dim):
    return lax.broadcasted_iota(I32, shape, dim)


def pack_kernel(a_ref, d_ref, q_ref, t_ref, cols_ref, mask_ref, agg_ref, agg2_ref, out_ref, meta):
    for i in range(N):
        out_ref[i * TILE:(i + 1) * TILE, :] = a_ref[i]
    for row, ref in ((ROW_D, d_ref), (ROW_Q, q_ref), (ROW_T, t_ref)):
        for w in range(N // 2):
            pair = jnp.concatenate([ref[2 * w], ref[2 * w + 1]], axis=1)
            out_ref[row:row + TILE, w * LANES:(w + 1) * LANES] = pair
    meta[...] = jnp.zeros_like(meta)
    meta[0:8, 0:8] = jnp.where(mask_ref[...] > 0, cols_ref[...], TRASH).astype(F32)
    meta[8:9, 0:8] = agg_ref[...].astype(F32)
    meta[9:10, 0:8] = agg2_ref[...].astype(F32)
    out_ref[ROW_META:ROWS, :] = meta[...].astype(BF16)


def pack(a, d, q, t, cols, mask, agg, agg2):
    return pl.pallas_call(
        pack_kernel,
        out_shape=jax.ShapeDtypeStruct((ROWS, W), BF16),
        in_specs=[VMEM] * 8,
        out_specs=VMEM,
        scratch_shapes=[pltpu.VMEM((16, W), F32)],
        compiler_params=params(),
    )(a, d, q, t, cols, mask, agg.reshape(1, N), agg2.reshape(1, N))


def halves(x):
    high = iota(x.shape, 1) >= TILE
    swapped = jnp.concatenate([x[:, TILE:], x[:, :TILE]], axis=1)
    zero = jnp.zeros_like(x)
    return (
        (jnp.where(high, zero, x), jnp.where(high, swapped, zero)),
        (jnp.where(high, zero, swapped), jnp.where(high, x, zero)),
    )


def window(index):
    return pl.ds(pl.multiple_of((index >> 1) * LANES, LANES), LANES)


def pick(variants, index):
    return jnp.where((index & 1) == 1, variants[1], variants[0])


def block_diagonal(row):
    block = iota(row.shape, 1) // TILE
    zero = jnp.zeros_like(row)
    return jnp.concatenate([jnp.where(block == i, row, zero) for i in range(N)], axis=0)


def to_scalars(pairs, sem):
    copies = [pltpu.make_async_copy(v, s, sem.at[n]) for n, (v, s) in enumerate(pairs)]
    for c in copies:
        c.start()
    for c in copies:
        c.wait()


def read_meta(tails, meta_v, meta_s, sem):
    for n, (ref, top) in enumerate(tails):
        meta_v[n] = ref[top:top + 16, 0:LANES].astype(F32).astype(I32)
    to_scalars([(meta_v.at[n], meta_s.at[n]) for n in range(len(tails))], sem)


def inside(slab, step, slabs):
    at = slab[0] + step
    return (at >= 0) & (at < slabs)


def place_q(out, ref, top, meta_s, n, valid=None):
    out[...] = jnp.zeros((W, W), BF16)
    for w in range(N // 2):
        sides = halves(ref[top:top + TILE, w * LANES:(w + 1) * LANES])
        for h in range(2):
            c = 2 * w + h
            g = meta_s[n, 8, c]
            out[c * TILE:(c + 1) * TILE, window(g)] = pick(sides[h], g)
    if valid is not None:
        @pl.when(jnp.logical_not(valid))
        def _():
            out[...] = jnp.zeros((W, W), BF16)


def pair_diagonal(pair):
    high = iota(pair.shape, 1) >= TILE
    zero = jnp.zeros_like(pair)
    return jnp.concatenate([jnp.where(high, zero, pair), jnp.where(high, pair, zero)], axis=0)


def place_a(refs, outs, sms, meta_s, metas, valids=None):
    def place_row(i, carry):
        rows = pl.ds(pl.multiple_of(i * TILE, TILE), TILE)
        for out in outs:
            out[rows, :] = jnp.zeros((TILE, WIDE), BF16)
        for w in range(N // 2):
            sides = [halves(ref[rows, w * LANES:(w + 1) * LANES]) for ref in refs]
            for h in range(2):
                for out, side, n in zip(outs, sides, metas):
                    c = meta_s[n, i, 2 * w + h]
                    if valids is not None:
                        c = jnp.where(valids[n], c, TRASH)
                    out[rows, window(c)] = out[rows, window(c)] + pick(side[h], c)
        return carry

    lax.fori_loop(0, N, place_row, 0)

    def smooth(w, carry):
        rows = pl.ds(pl.multiple_of(w * LANES, LANES), LANES)
        for ref, out, sm in zip(refs, outs, sms):
            diag = pair_diagonal(ref[ROW_D:ROW_D + TILE, rows])
            sm[rows, :] = (DAMPING * dot(diag, out[rows, 0:3 * W])).astype(BF16)
        return carry

    lax.fori_loop(0, N // 2, smooth, 0)


def write_term(term, n, tpt, c, ref, top):
    lhs = dot(tpt[...], c.astype(BF16)).astype(BF16)
    for w in range(N // 2):
        diag = pair_diagonal(ref[top:top + TILE, w * LANES:(w + 1) * LANES])
        at = n * W + w * LANES
        term[:, at:at + LANES] = dot(lhs[:, w * LANES:(w + 1) * LANES], diag).astype(BF16)


def write_ids(term, count, ids_v, meta_v, order):
    ids_v[...] = jnp.zeros_like(ids_v)
    for row, n in enumerate(order):
        ids_v[row:row + 1, :] = meta_v[n, 9:10, :].astype(F32)
    for q in range(GROUPS):
        term[q * CHUNK:(q + 1) * CHUNK, count * W:] = ids_v[...].astype(BF16)


def block(j):
    return slice(j * W, (j + 1) * W)


def own_kernel(own, rap, sm, qs, r0, tpt, ad, meta_v, meta_s, sem):
    read_meta([(own, ROW_META)], meta_v, meta_s, sem)
    place_q(qs, own, ROW_Q, meta_s, 0)
    place_a((own,), (ad,), (sm,), meta_s, (0,))
    r0[...] = (qs[...].astype(F32) - dot(sm[:, block(1)], qs[...])).astype(BF16)
    turned = r0[...].T
    for j in range(3):
        rap[:, block(j)] = dot(turned, ad[:, block(j)])
    left = block_diagonal(own[ROW_T:ROW_T + TILE, :])
    lead = iota((W, W), 0)
    target = ((lead >> 2) & 7) * TILE + (lead >> 5) * PART + (lead & 3)
    turn = (target == iota((W, W), 1)).astype(F32).astype(BF16)
    tpt[...] = lax.dot_general(turn, left, (((1,), (1,)), ((), ())), preferred_element_type=F32).astype(BF16)


def start_own(own):
    shape = jax.ShapeDtypeStruct
    return pl.pallas_call(
        own_kernel,
        out_shape=(
            shape((W, 3 * W), F32), shape((W, 3 * W), BF16), shape((W, W), BF16),
            shape((W, W), BF16), shape((W, W), BF16),
        ),
        in_specs=[VMEM],
        out_specs=(VMEM,) * 5,
        scratch_shapes=[
            pltpu.VMEM((W, WIDE), BF16),
            pltpu.VMEM((1, 16, LANES), I32),
            pltpu.SMEM((1, 16, LANES), I32),
            pltpu.SemaphoreType.DMA((1,)),
        ],
        compiler_params=params(),
        cost_estimate=pl.CostEstimate(flops=3_000_000_000, bytes_accessed=6 << 20, transcendentals=0),
    )(own)


def fetch(pairs, sem):
    copies = [pltpu.make_async_copy(src, dst, sem.at[n]) for n, (src, dst) in enumerate(pairs)]
    for c in copies:
        c.start()
    return copies


def near_kernel(slabs, slab, m1, p1, rap_h, sm_h, qs_h, r0_h, tpt_h, own,
                c_ref, term_ref, part_h, ra_h, smo_h, m1_tail, p1_tail,
                ad0, ad2, sm0, sm1, sm2, qs1, rm, r0, rp, tpt, rap, ra, part, cbuf, tbuf,
                meta_v, meta_s, sem, in_sem, out_sem):
    ins = fetch(((qs_h, qs1), (rap_h, rap), (r0_h, r0), (tpt_h, tpt), (sm_h, sm1)), in_sem)
    outs = []

    def send(src, dst):
        outs.append(pltpu.make_async_copy(src, dst, out_sem.at[len(outs)]))
        outs[-1].start()

    send(m1.at[ROW_Q:ROWS, :], m1_tail)
    send(p1.at[ROW_Q:ROWS, :], p1_tail)
    read_meta([(m1, ROW_META), (p1, ROW_META)], meta_v, meta_s, sem)
    valids = (inside(slab, -1, slabs), inside(slab, 1, slabs))
    place_a((m1, p1), (ad0, ad2), (sm0, sm2), meta_s, (0, 1), valids)
    send(sm0.at[:, block(0)], smo_h.at[:, block(0)])
    send(sm2.at[:, W:3 * W], smo_h.at[:, W:3 * W])
    for copy in ins:
        copy.wait()

    rm[...] = (-dot(sm0[:, block(2)], qs1[...])).astype(BF16)
    rp[...] = (-dot(sm2[:, block(0)], qs1[...])).astype(BF16)
    before, after = rm[...].T, rp[...].T
    ra[:, block(0)] = dot(before, ad0[:, block(0)]).astype(BF16)
    ra[:, block(1)] = (dot(before, ad0[:, block(1)]) + rap[:, block(0)]).astype(BF16)
    ra[:, block(2)] = (dot(before, ad0[:, block(2)]) + dot(after, ad2[:, block(0)]) + rap[:, block(1)]).astype(BF16)
    ra[:, block(3)] = (dot(after, ad2[:, block(1)]) + rap[:, block(2)]).astype(BF16)
    ra[:, block(4)] = dot(after, ad2[:, block(2)]).astype(BF16)
    send(ra, ra_h)

    lead = ra[:, block(1)]
    part[...] = lead.astype(F32) - dot(lead, sm0[:, block(1)]) - dot(ra[:, block(2)], sm1[:, block(0)])
    send(part, part_h)
    cbuf[...] = dot(ra[:, block(1)], rm[...]) + dot(ra[:, block(2)], r0[...]) + dot(ra[:, block(3)], rp[...])
    send(cbuf, c_ref.at[:, block(3)])
    write_term(tbuf, 0, tpt, cbuf[...], own, TAIL_T)
    send(tbuf, term_ref.at[:, block(0)])
    for copy in outs:
        copy.wait()


def near(slab, m1, p1, rap, sm, qs, r0, tpt, own):
    shape = jax.ShapeDtypeStruct
    return pl.pallas_call(
        functools.partial(near_kernel, lax.axis_size("slab")),
        grid=(1,),
        out_shape=(
            shape((W, 7 * W), F32), shape((W, 2 * W + LANES), BF16), shape((W, W), F32),
            shape((W, 5 * W), BF16), shape((W, 3 * W), BF16), shape((144, W), BF16), shape((144, W), BF16),
        ),
        in_specs=[SMEM, VMEM, VMEM] + [ANY] * 5 + [TAIL],
        out_specs=(ANY,) * 7,
        scratch_shapes=[pltpu.VMEM((W, WIDE), BF16)] * 2
        + [pltpu.VMEM((W, 3 * W), BF16)] * 3
        + [pltpu.VMEM((W, W), BF16)] * 5
        + [
            pltpu.VMEM((W, 3 * W), F32),
            pltpu.VMEM((W, 5 * W), BF16),
            pltpu.VMEM((W, W), F32),
            pltpu.VMEM((W, W), F32),
            pltpu.VMEM((W, W), BF16),
            pltpu.VMEM((2, 16, LANES), I32),
            pltpu.SMEM((2, 16, LANES), I32),
            pltpu.SemaphoreType.DMA((2,)),
            pltpu.SemaphoreType.DMA((5,)),
            pltpu.SemaphoreType.DMA((8,)),
        ],
        compiler_params=params(),
        cost_estimate=pl.CostEstimate(flops=9_000_000_000, bytes_accessed=14 << 20, transcendentals=0),
    )(slab, m1, p1, rap, sm, qs, r0, tpt, own)


def smooth_far(ref, flat, sm, meta_s, n, valid):
    for w in range(N // 2):
        rows = slice(w * LANES, (w + 1) * LANES)
        diag = pair_diagonal(ref[ROW_D:ROW_D + TILE, rows])
        flat[rows, :] = (DAMPING * dot(diag, ref[rows, :])).astype(BF16)
    tops = (0, W // 2)

    def place_row(i, carry):
        starts = [pl.ds(pl.multiple_of(top + i * TILE, TILE), TILE) for top in tops]
        for rows in starts:
            sm[rows, :] = jnp.zeros((TILE, WIDE), BF16)
        for w in range(N // 2):
            sides = [halves(flat[rows, w * LANES:(w + 1) * LANES]) for rows in starts]
            for h in range(2):
                for d, rows in enumerate(starts):
                    c = jnp.where(valid, meta_s[n, i + d * N // 2, 2 * w + h], TRASH)
                    sm[rows, window(c)] = sm[rows, window(c)] + pick(sides[d][h], c)
        return carry

    lax.fori_loop(0, N // 2, place_row, 0)


def second_kernel(slabs, slab, m2_h, m1, own, part_h, ra_h, tpt_h, c_in, term_in, c_ref, term_ref, smm_out,
                  m2, flat, smm, qs, pw, part, ra, tpt, cbuf, tbuf, meta_v, meta_s, ids_v, sem, in_sem, out_sem):
    del c_in, term_in
    landed = pltpu.make_async_copy(m2_h, m2, in_sem.at[3])
    landed.start()
    ins = fetch(((part_h, part), (ra_h.at[:, block(0)], ra), (tpt_h, tpt)), in_sem)
    landed.wait()
    read_meta([(m2, ROW_META), (m1, TAIL_META), (own, TAIL_META)], meta_v, meta_s, sem)
    write_ids(tbuf, 1, ids_v, meta_v, (2, 2, 1))
    smooth_far(m2, flat, smm, meta_s, 0, inside(slab, -2, slabs))
    place_q(qs, m1, TAIL_Q, meta_s, 1, inside(slab, -1, slabs))
    for copy in ins:
        copy.wait()
    pw[...] = (part[...] - dot(ra[...], smm[:, block(2)])).astype(BF16)
    cbuf[...] = dot(pw[...], qs[...])
    out = pltpu.make_async_copy(cbuf, c_ref.at[:, block(2)], out_sem.at[0])
    out.start()
    write_term(tbuf, 0, tpt, cbuf[...], m1, TAIL_T)
    sent = pltpu.make_async_copy(tbuf, term_ref.at[:, W:], out_sem.at[1])
    sent.start()
    smm_out[...] = smm[:, 0:2 * W]
    out.wait()
    sent.wait()


def second(slab, m2, m1, own, part, ra, tpt, c, term):
    shape = jax.ShapeDtypeStruct
    return pl.pallas_call(
        functools.partial(second_kernel, lax.axis_size("slab")),
        out_shape=(shape((W, 7 * W), F32), shape((W, 2 * W + LANES), BF16), shape((W, 2 * W), BF16)),
        grid=(1,),
        in_specs=[SMEM, ANY, TAIL, TAIL] + [ANY] * 5,
        out_specs=(ANY, ANY, VMEM),
        input_output_aliases={7: 0, 8: 1},
        scratch_shapes=[
            pltpu.VMEM((ROWS, W), BF16),
            pltpu.VMEM((W, W), BF16),
            pltpu.VMEM((W, WIDE), BF16),
            pltpu.VMEM((W, W), BF16),
            pltpu.VMEM((W, W), BF16),
            pltpu.VMEM((W, W), F32),
            pltpu.VMEM((W, W), BF16),
            pltpu.VMEM((W, W), BF16),
            pltpu.VMEM((W, W), F32),
            pltpu.VMEM((W, W + LANES), BF16),
            pltpu.VMEM((3, 16, LANES), I32),
            pltpu.SMEM((3, 16, LANES), I32),
            pltpu.VMEM((CHUNK, LANES), F32),
            pltpu.SemaphoreType.DMA((3,)),
            pltpu.SemaphoreType.DMA((4,)),
            pltpu.SemaphoreType.DMA((2,)),
        ],
        compiler_params=params(),
        cost_estimate=pl.CostEstimate(flops=4_000_000_000, bytes_accessed=8 << 20, transcendentals=0),
    )(slab, m2, m1, own, part, ra, tpt, c, term)


def third_kernel(slabs, slab, p2, p1, m3, m2, p3, own, sm_h, smm_h, smo_h, ra_h, tpt_h, c_in, c_ref, term,
                 flat, smp, qs, pw, cbuf, sm1, smm, smo, ra, tpt, meta_v, meta_s, ids_v, sem, in_sem, out_sem):
    del c_in
    ins = fetch(((sm_h.at[:, block(2)], sm1), (smm_h, smm), (smo_h, smo), (ra_h, ra), (tpt_h, tpt)), in_sem)
    read_meta([(p2, ROW_META)] + [(ref, TAIL_META) for ref in (p1, m2, m3, p3, own)], meta_v, meta_s, sem)
    write_ids(term, 5, ids_v, meta_v, (5, 1, 2, 0, 3, 4))
    smooth_far(p2, flat, smp, meta_s, 0, inside(slab, 2, slabs))
    for copy in ins:
        copy.wait()
    outs = []

    def columns(n, value, o, ref, top, at):
        pw[...] = value.astype(BF16)
        place_q(qs, ref, top, meta_s, at, inside(slab, o - 3, slabs))
        cbuf[n] = dot(pw[...], qs[...])
        outs.append(pltpu.make_async_copy(cbuf.at[n], c_ref.at[:, block(o)], out_sem.at[n]))
        outs[-1].start()
        write_term(term, n, tpt, cbuf[n], ref, top + TILE)

    first, last = ra[:, block(0)], ra[:, block(4)]
    near = ra[:, block(3)]
    value = near.astype(F32) - dot(near, smo[:, block(1)]) - dot(ra[:, block(2)], sm1[...])
    columns(0, value - dot(last, smp[:, block(0)]), 4, p1, TAIL_Q, 1)
    value = first.astype(F32) - dot(first, smm[:, block(1)]) - dot(ra[:, block(1)], smo[:, block(0)])
    columns(1, value, 1, m2, TAIL_Q, 2)
    value = last.astype(F32) - dot(last, smp[:, block(1)]) - dot(near, smo[:, block(2)])
    columns(2, value, 5, p2, ROW_Q, 0)
    columns(3, -dot(first, smm[:, block(0)]), 0, m3, TAIL_Q, 3)
    columns(4, -dot(last, smp[:, block(2)]), 6, p3, TAIL_Q, 4)
    for out in outs:
        out.wait()


def third(slab, p2, p1, m3, m2, p3, own, sm, smm, smo, ra, tpt, c):
    shape = jax.ShapeDtypeStruct
    return pl.pallas_call(
        functools.partial(third_kernel, lax.axis_size("slab")),
        out_shape=(shape((W, 7 * W), F32), shape((W, 5 * W + LANES), BF16)),
        grid=(1,),
        in_specs=[SMEM, VMEM, TAIL, VMEM, TAIL, VMEM, TAIL] + [ANY] * 6,
        out_specs=(ANY, VMEM),
        input_output_aliases={12: 0},
        scratch_shapes=[
            pltpu.VMEM((W, W), BF16),
            pltpu.VMEM((W, WIDE), BF16),
            pltpu.VMEM((W, W), BF16),
            pltpu.VMEM((W, W), BF16),
            pltpu.VMEM((5, W, W), F32),
            pltpu.VMEM((W, W), BF16),
            pltpu.VMEM((W, 2 * W), BF16),
            pltpu.VMEM((W, 3 * W), BF16),
            pltpu.VMEM((W, 5 * W), BF16),
            pltpu.VMEM((W, W), BF16),
            pltpu.VMEM((6, 16, LANES), I32),
            pltpu.SMEM((6, 16, LANES), I32),
            pltpu.VMEM((CHUNK, LANES), F32),
            pltpu.SemaphoreType.DMA((6,)),
            pltpu.SemaphoreType.DMA((5,)),
            pltpu.SemaphoreType.DMA((5,)),
        ],
        compiler_params=params(),
        cost_estimate=pl.CostEstimate(flops=7_000_000_000, bytes_accessed=18 << 20, transcendentals=0),
    )(slab, p2, p1, m3, m2, p3, own, sm, smm, smo, ra, tpt, c)


def gather_pieces(count, x_h, x_ref, lows, highs, ids_v, ids_s, sem):
    landed = pltpu.make_async_copy(x_h, x_ref, sem.at[1])
    landed.start()
    for y in lows + highs:
        y[...] = jnp.zeros_like(y)
    landed.wait()
    for p in range(GROUPS):
        ids_v[p] = x_ref[p, 0:8, count * W:].astype(F32).astype(I32)
    to_scalars([(ids_v, ids_s)], sem)

    def one(p, carry):
        rows = pl.ds(pl.multiple_of(p * CHUNK, CHUNK), CHUNK)
        for w in range(N // 2):
            sides = [
                [halves(x_ref[p + d, :, o * W + w * LANES:o * W + (w + 1) * LANES]) for d in (0, GROUPS // 2)]
                for o in range(count)
            ]
            for h in range(2):
                for o in range(count):
                    for y, side, d in ((lows[o], sides[o][0], 0), (highs[o], sides[o][1], GROUPS // 2)):
                        g = ids_s[p + d, 1 + o, 2 * w + h]
                        y[rows, window(g)] = y[rows, window(g)] + pick(side[h], g)
        return carry

    lax.fori_loop(0, GROUPS // 2, one, 0)


def add_pieces(count, first, takes, lows, highs, out_ref):
    for o in range(count):
        total = None
        for cq in range(4):
            cols = slice(cq * QUARTER, (cq + 1) * QUARTER)
            piece = dot(takes[cq, :, 0:256], lows[o][:, cols]) + dot(takes[cq, :, 256:W], highs[o][:, cols])
            total = piece if total is None else total + piece
        out_ref[:, (first + o) * QUARTER:(first + o + 1) * QUARTER] = total.astype(BF16)


def merge_first_kernel(count, x_h, out_ref, takes, *rest):
    lows, highs, (x_ref, ids_v, ids_s, sem) = rest[:count], rest[count:2 * count], rest[2 * count:]
    gather_pieces(count, x_h, x_ref, lows, highs, ids_v, ids_s, sem)
    groups = jnp.concatenate([ids_v[p, 0:1, :] for p in range(GROUPS)], axis=0).astype(F32).astype(BF16)
    spread = (((iota((LANES, W), 1) >> 2) & 7) == iota((LANES, W), 0)).astype(F32).astype(BF16)
    each = dot(groups, spread)
    mine = (iota((GROUPS, W), 1) >> 5) == iota((GROUPS, W), 0)
    group = jnp.sum(jnp.where(mine, each, 0.0), axis=0, keepdims=True).astype(I32)
    row, col = iota((256, W), 0), iota((256, W), 1)
    hit = ((row >> 4) == group) & ((row & 3) == (col & 3))
    for cq in range(4):
        takes[cq] = (hit & (((row >> 2) & 3) == cq)).astype(F32).astype(BF16)
    add_pieces(count, 0, takes, lows, highs, out_ref)


def merge_last_kernel(count, x_h, done, takes, out_ref, *rest):
    lows, highs, (x_ref, ids_v, ids_s, sem) = rest[:count], rest[count:2 * count], rest[2 * count:]
    out_ref[:, 0:done.shape[1]] = done[...]
    gather_pieces(count, x_h, x_ref, lows, highs, ids_v, ids_s, sem)
    add_pieces(count, done.shape[1] // QUARTER, takes, lows, highs, out_ref)


def merge(x, done=None, takes=None):
    count = x.shape[2] // W
    shape = jax.ShapeDtypeStruct
    first = done is None
    earlier = 0 if first else done.shape[1] // QUARTER
    out = shape((256, (earlier + count) * QUARTER), BF16)
    return pl.pallas_call(
        functools.partial(merge_first_kernel if first else merge_last_kernel, count),
        out_shape=(out, shape((4, 256, W), BF16)) if first else out,
        in_specs=[ANY] if first else [ANY, VMEM, VMEM],
        out_specs=(VMEM, VMEM) if first else VMEM,
        scratch_shapes=[pltpu.VMEM((GROUPS * CHUNK // 2, GROUPS * TILE), BF16)] * (2 * count)
        + [
            pltpu.VMEM(x.shape, BF16),
            pltpu.VMEM((GROUPS, 8, LANES), I32),
            pltpu.SMEM((GROUPS, 8, LANES), I32),
            pltpu.SemaphoreType.DMA((2,)),
        ],
        compiler_params=params(),
        cost_estimate=pl.CostEstimate(flops=1_000_000_000 * count, bytes_accessed=count << 20, transcendentals=0),
    )(*((x,) if first else (x, done, takes)))


def finish_kernel(order, x_ref, out_h, out_ref, sem):
    row, col = iota((TILE, 256), 0), iota((TILE, 256), 1)
    same = ((row >> 2) == (col >> 4)) & ((row & 3) == (col & 3))
    takes = [(same & (((col >> 2) & 3) == cq)).astype(F32).astype(BF16) for cq in range(4)]
    copies = []
    for n, o in enumerate(order):
        for cq in range(4):
            at = o * 4 * QUARTER + cq * QUARTER
            out_ref[0, :, at:at + QUARTER] = dot(takes[cq], x_ref[:, n * QUARTER:(n + 1) * QUARTER])
        cols = slice(o * 4 * QUARTER, (o + 1) * 4 * QUARTER)
        copies.append(pltpu.make_async_copy(out_ref.at[:, :, cols], out_h.at[:, :, cols], sem.at[n]))
        copies[n].start()
    for copy in copies:
        copy.wait()


def finish(order, x):
    shape = (1, TILE, DENSE)
    return pl.pallas_call(
        functools.partial(finish_kernel, order),
        out_shape=jax.ShapeDtypeStruct(shape, F32),
        in_specs=[VMEM],
        out_specs=ANY,
        scratch_shapes=[pltpu.VMEM(shape, F32), pltpu.SemaphoreType.DMA((len(order),))],
        compiler_params=params(),
    )(x)


def along(block, step):
    count = lax.axis_size("slab")
    route = [(i, (i + step) % count) for i in range(count)]
    return lax.ppermute(block, "slab", route)


def exchange(term):
    return lax.all_to_all(term.reshape(GROUPS, CHUNK, term.shape[1]), "piece", 0, 0)


def hand_over(dense):
    back = lax.all_to_all(dense.reshape(GROUPS, 16, dense.shape[1]), "piece", 0, 0)
    return back.reshape(256, dense.shape[1])


def device_part(fine_tiles, fine_cols, bond_mask, diag_inv, tentative, aggregate, tentative_two, aggregate_two):
    own = pack(fine_tiles, diag_inv, tentative, tentative_two, fine_cols, bond_mask, aggregate, aggregate_two)
    m1, p1 = along(own, 1), along(own, -1)
    slab = lax.axis_index("slab").astype(I32).reshape(1)
    rap, sm, qs, r0, tpt = start_own(own)
    m2 = along(m1, 1)
    p2 = along(p1, -1)
    c, term, part, ra, smo, m1_tail, p1_tail = near(slab, m1, p1, rap, sm, qs, r0, tpt, own)
    m3 = along(m1_tail, 2)
    p3 = along(p1_tail, -2)
    c, term, smm = second(slab, m2, m1, own, part, ra, tpt, c, term)
    got = exchange(term)
    c, term = third(slab, p2, p1, m3, m2, p3, own, sm, smm, smo, ra, tpt, c)
    last = exchange(term)
    done, takes = merge(got)
    level_two = finish((3, 2, 4, 1, 5, 0, 6), hand_over(merge(last, done, takes)))
    return c.reshape(N, TILE, 7 * W), level_two


def solution(mesh):
    both = ("slab", "piece")
    placed = (
        P(both, None, None), P(both, None), P(both, None), P(both, None, None),
        P(both, None, None), P(both), P(both, None, None), P(both),
    )
    return jax.shard_map(
        device_part,
        mesh=mesh,
        in_specs=placed,
        out_specs=(P(both, None, None), P(both, None, None)),
        check_vma=False,
    )
```

```python
import functools

import jax
import jax.numpy as jnp
from jax import lax
from jax.experimental import pallas as pl
from jax.experimental.pallas import tpu as pltpu
from jax.sharding import PartitionSpec as P


DAMPING = 2.0 / 3.0
TILE = 64
N = 8
W = N * TILE
LANES = 128
TRASH = 3 * N
WIDE = 3 * W + LANES
ROW_D, ROW_Q, ROW_T, ROW_META, ROWS = W, W + 64, W + 128, W + 192, W + 208
ANY = pl.BlockSpec(memory_space=pl.ANY)
VMEM = pl.BlockSpec(memory_space=pltpu.VMEM)
SMEM = pl.BlockSpec(memory_space=pltpu.SMEM)
BF16, F32, I32 = jnp.bfloat16, jnp.float32, jnp.int32
GROUPS = 16
PART = 4
CHUNK = N * PART
DENSE = 7 * GROUPS * TILE
QUARTER = GROUPS * TILE // 4
TAIL = pl.BlockSpec((144, W), lambda i: (ROW_Q // 144, 0))
TAIL_Q, TAIL_T, TAIL_META = 0, 64, 128


def params():
    return pltpu.CompilerParams(vmem_limit_bytes=67_043_328)


def dot(a, b):
    return jnp.dot(a, b, preferred_element_type=F32)


def iota(shape, dim):
    return lax.broadcasted_iota(I32, shape, dim)


def pack_kernel(a_ref, d_ref, q_ref, t_ref, cols_ref, mask_ref, agg_ref, agg2_ref, out_ref, meta):
    for i in range(N):
        out_ref[i * TILE:(i + 1) * TILE, :] = a_ref[i]
    for row, ref in ((ROW_D, d_ref), (ROW_Q, q_ref), (ROW_T, t_ref)):
        for w in range(N // 2):
            pair = jnp.concatenate([ref[2 * w], ref[2 * w + 1]], axis=1)
            out_ref[row:row + TILE, w * LANES:(w + 1) * LANES] = pair
    meta[...] = jnp.zeros_like(meta)
    meta[0:8, 0:8] = jnp.where(mask_ref[...] > 0, cols_ref[...], TRASH).astype(F32)
    meta[8:9, 0:8] = agg_ref[...].astype(F32)
    meta[9:10, 0:8] = agg2_ref[...].astype(F32)
    out_ref[ROW_META:ROWS, :] = meta[...].astype(BF16)


def pack(a, d, q, t, cols, mask, agg, agg2):
    return pl.pallas_call(
        pack_kernel,
        out_shape=jax.ShapeDtypeStruct((ROWS, W), BF16),
        in_specs=[VMEM] * 8,
        out_specs=VMEM,
        scratch_shapes=[pltpu.VMEM((16, W), F32)],
        compiler_params=params(),
    )(a, d, q, t, cols, mask, agg.reshape(1, N), agg2.reshape(1, N))


def halves(x):
    high = iota(x.shape, 1) >= TILE
    swapped = jnp.concatenate([x[:, TILE:], x[:, :TILE]], axis=1)
    zero = jnp.zeros_like(x)
    return (
        (jnp.where(high, zero, x), jnp.where(high, swapped, zero)),
        (jnp.where(high, zero, swapped), jnp.where(high, x, zero)),
    )


def window(index):
    return pl.ds(pl.multiple_of((index >> 1) * LANES, LANES), LANES)


def pick(variants, index):
    return jnp.where((index & 1) == 1, variants[1], variants[0])


def block_diagonal(row):
    block = iota(row.shape, 1) // TILE
    zero = jnp.zeros_like(row)
    return jnp.concatenate([jnp.where(block == i, row, zero) for i in range(N)], axis=0)


def to_scalars(pairs, sem):
    copies = [pltpu.make_async_copy(v, s, sem.at[n]) for n, (v, s) in enumerate(pairs)]
    for c in copies:
        c.start()
    for c in copies:
        c.wait()


def read_meta(tails, meta_v, meta_s, sem):
    for n, (ref, top) in enumerate(tails):
        meta_v[n] = ref[top:top + 16, 0:LANES].astype(F32).astype(I32)
    to_scalars([(meta_v.at[n], meta_s.at[n]) for n in range(len(tails))], sem)


def inside(slab, step, slabs):
    at = slab[0] + step
    return (at >= 0) & (at < slabs)


def place_q(out, ref, top, meta_s, n, valid=None):
    out[...] = jnp.zeros((W, W), BF16)
    for w in range(N // 2):
        sides = halves(ref[top:top + TILE, w * LANES:(w + 1) * LANES])
        for h in range(2):
            c = 2 * w + h
            g = meta_s[n, 8, c]
            out[c * TILE:(c + 1) * TILE, window(g)] = pick(sides[h], g)
    if valid is not None:
        @pl.when(jnp.logical_not(valid))
        def _():
            out[...] = jnp.zeros((W, W), BF16)


def pair_diagonal(pair):
    high = iota(pair.shape, 1) >= TILE
    zero = jnp.zeros_like(pair)
    return jnp.concatenate([jnp.where(high, zero, pair), jnp.where(high, pair, zero)], axis=0)


def place_a(refs, outs, sms, meta_s, metas, valids=None):
    def place_row(i, carry):
        rows = pl.ds(pl.multiple_of(i * TILE, TILE), TILE)
        for out in outs:
            out[rows, :] = jnp.zeros((TILE, WIDE), BF16)
        for w in range(N // 2):
            sides = [halves(ref[rows, w * LANES:(w + 1) * LANES]) for ref in refs]
            for h in range(2):
                for out, side, n in zip(outs, sides, metas):
                    c = meta_s[n, i, 2 * w + h]
                    if valids is not None:
                        c = jnp.where(valids[n], c, TRASH)
                    out[rows, window(c)] = out[rows, window(c)] + pick(side[h], c)
        return carry

    lax.fori_loop(0, N, place_row, 0)

    def smooth(w, carry):
        rows = pl.ds(pl.multiple_of(w * LANES, LANES), LANES)
        for ref, out, sm in zip(refs, outs, sms):
            diag = pair_diagonal(ref[ROW_D:ROW_D + TILE, rows])
            sm[rows, :] = (DAMPING * dot(diag, out[rows, 0:3 * W])).astype(BF16)
        return carry

    lax.fori_loop(0, N // 2, smooth, 0)


def write_term(term, n, tpt, c, ref, top):
    lhs = dot(tpt[...], c.astype(BF16)).astype(BF16)
    for w in range(N // 2):
        diag = pair_diagonal(ref[top:top + TILE, w * LANES:(w + 1) * LANES])
        at = n * W + w * LANES
        term[:, at:at + LANES] = dot(lhs[:, w * LANES:(w + 1) * LANES], diag).astype(BF16)


def write_ids(term, count, ids_v, meta_v, order):
    ids_v[...] = jnp.zeros_like(ids_v)
    for row, n in enumerate(order):
        ids_v[row:row + 1, :] = meta_v[n, 9:10, :].astype(F32)
    for q in range(GROUPS):
        term[q * CHUNK:(q + 1) * CHUNK, count * W:] = ids_v[...].astype(BF16)


def block(j):
    return slice(j * W, (j + 1) * W)


def own_kernel(own, rap, sm, qs, r0, tpt, ad, meta_v, meta_s, sem):
    read_meta([(own, ROW_META)], meta_v, meta_s, sem)
    place_q(qs, own, ROW_Q, meta_s, 0)
    place_a((own,), (ad,), (sm,), meta_s, (0,))
    r0[...] = (qs[...].astype(F32) - dot(sm[:, block(1)], qs[...])).astype(BF16)
    turned = r0[...].T
    for j in range(3):
        rap[:, block(j)] = dot(turned, ad[:, block(j)])
    left = block_diagonal(own[ROW_T:ROW_T + TILE, :])
    lead = iota((W, W), 0)
    target = ((lead >> 2) & 7) * TILE + (lead >> 5) * PART + (lead & 3)
    turn = (target == iota((W, W), 1)).astype(F32).astype(BF16)
    tpt[...] = lax.dot_general(turn, left, (((1,), (1,)), ((), ())), preferred_element_type=F32).astype(BF16)


def start_own(own):
    shape = jax.ShapeDtypeStruct
    return pl.pallas_call(
        own_kernel,
        out_shape=(
            shape((W, 3 * W), F32), shape((W, 3 * W), BF16), shape((W, W), BF16),
            shape((W, W), BF16), shape((W, W), BF16),
        ),
        in_specs=[VMEM],
        out_specs=(VMEM,) * 5,
        scratch_shapes=[
            pltpu.VMEM((W, WIDE), BF16),
            pltpu.VMEM((1, 16, LANES), I32),
            pltpu.SMEM((1, 16, LANES), I32),
            pltpu.SemaphoreType.DMA((1,)),
        ],
        compiler_params=params(),
        cost_estimate=pl.CostEstimate(flops=3_000_000_000, bytes_accessed=6 << 20, transcendentals=0),
    )(own)


def fetch(pairs, sem):
    copies = [pltpu.make_async_copy(src, dst, sem.at[n]) for n, (src, dst) in enumerate(pairs)]
    for c in copies:
        c.start()
    return copies


def near_kernel(slabs, slab, m1, p1, rap_h, sm_h, qs_h, r0_h, tpt_h, own,
                c_ref, term_ref, part_h, ra_h, smo_h, m1_tail, p1_tail,
                ad0, ad2, sm0, sm1, sm2, qs1, rm, r0, rp, tpt, rap, ra, part, cbuf, tbuf,
                meta_v, meta_s, sem, in_sem, out_sem):
    ins = fetch(((qs_h, qs1), (rap_h, rap), (r0_h, r0), (tpt_h, tpt), (sm_h, sm1)), in_sem)
    outs = []

    def send(src, dst):
        outs.append(pltpu.make_async_copy(src, dst, out_sem.at[len(outs)]))
        outs[-1].start()

    send(m1.at[ROW_Q:ROWS, :], m1_tail)
    send(p1.at[ROW_Q:ROWS, :], p1_tail)
    read_meta([(m1, ROW_META), (p1, ROW_META)], meta_v, meta_s, sem)
    valids = (inside(slab, -1, slabs), inside(slab, 1, slabs))
    place_a((m1, p1), (ad0, ad2), (sm0, sm2), meta_s, (0, 1), valids)
    send(sm0.at[:, block(0)], smo_h.at[:, block(0)])
    send(sm2.at[:, W:3 * W], smo_h.at[:, W:3 * W])
    for copy in ins:
        copy.wait()

    rm[...] = (-dot(sm0[:, block(2)], qs1[...])).astype(BF16)
    rp[...] = (-dot(sm2[:, block(0)], qs1[...])).astype(BF16)
    before, after = rm[...].T, rp[...].T
    ra[:, block(0)] = dot(before, ad0[:, block(0)]).astype(BF16)
    ra[:, block(1)] = (dot(before, ad0[:, block(1)]) + rap[:, block(0)]).astype(BF16)
    ra[:, block(2)] = (dot(before, ad0[:, block(2)]) + dot(after, ad2[:, block(0)]) + rap[:, block(1)]).astype(BF16)
    ra[:, block(3)] = (dot(after, ad2[:, block(1)]) + rap[:, block(2)]).astype(BF16)
    ra[:, block(4)] = dot(after, ad2[:, block(2)]).astype(BF16)
    send(ra, ra_h)

    lead = ra[:, block(1)]
    part[...] = lead.astype(F32) - dot(lead, sm0[:, block(1)]) - dot(ra[:, block(2)], sm1[:, block(0)])
    send(part, part_h)
    cbuf[...] = dot(ra[:, block(1)], rm[...]) + dot(ra[:, block(2)], r0[...]) + dot(ra[:, block(3)], rp[...])
    send(cbuf, c_ref.at[:, block(3)])
    write_term(tbuf, 0, tpt, cbuf[...], own, TAIL_T)
    send(tbuf, term_ref.at[:, block(0)])
    for copy in outs:
        copy.wait()


def near(slab, m1, p1, rap, sm, qs, r0, tpt, own):
    shape = jax.ShapeDtypeStruct
    return pl.pallas_call(
        functools.partial(near_kernel, lax.axis_size("slab")),
        grid=(1,),
        out_shape=(
            shape((W, 7 * W), F32), shape((W, 2 * W + LANES), BF16), shape((W, W), F32),
            shape((W, 5 * W), BF16), shape((W, 3 * W), BF16), shape((144, W), BF16), shape((144, W), BF16),
        ),
        in_specs=[SMEM, VMEM, VMEM] + [ANY] * 5 + [TAIL],
        out_specs=(ANY,) * 7,
        scratch_shapes=[pltpu.VMEM((W, WIDE), BF16)] * 2
        + [pltpu.VMEM((W, 3 * W), BF16)] * 3
        + [pltpu.VMEM((W, W), BF16)] * 5
        + [
            pltpu.VMEM((W, 3 * W), F32),
            pltpu.VMEM((W, 5 * W), BF16),
            pltpu.VMEM((W, W), F32),
            pltpu.VMEM((W, W), F32),
            pltpu.VMEM((W, W), BF16),
            pltpu.VMEM((2, 16, LANES), I32),
            pltpu.SMEM((2, 16, LANES), I32),
            pltpu.SemaphoreType.DMA((2,)),
            pltpu.SemaphoreType.DMA((5,)),
            pltpu.SemaphoreType.DMA((8,)),
        ],
        compiler_params=params(),
        cost_estimate=pl.CostEstimate(flops=9_000_000_000, bytes_accessed=14 << 20, transcendentals=0),
    )(slab, m1, p1, rap, sm, qs, r0, tpt, own)


def smooth_far(ref, flat, sm, meta_s, n, valid):
    for w in range(N // 2):
        rows = slice(w * LANES, (w + 1) * LANES)
        diag = pair_diagonal(ref[ROW_D:ROW_D + TILE, rows])
        flat[rows, :] = (DAMPING * dot(diag, ref[rows, :])).astype(BF16)
    tops = (0, W // 2)

    def place_row(i, carry):
        starts = [pl.ds(pl.multiple_of(top + i * TILE, TILE), TILE) for top in tops]
        for rows in starts:
            sm[rows, :] = jnp.zeros((TILE, WIDE), BF16)
        for w in range(N // 2):
            sides = [halves(flat[rows, w * LANES:(w + 1) * LANES]) for rows in starts]
            for h in range(2):
                for d, rows in enumerate(starts):
                    c = jnp.where(valid, meta_s[n, i + d * N // 2, 2 * w + h], TRASH)
                    sm[rows, window(c)] = sm[rows, window(c)] + pick(sides[d][h], c)
        return carry

    lax.fori_loop(0, N // 2, place_row, 0)


def second_kernel(slabs, slab, m2, m1, own, part_h, ra_h, tpt_h, c_in, term_in, c_ref, term_ref, smm_out,
                  flat, smm, qs, pw, part, ra, tpt, cbuf, tbuf, meta_v, meta_s, ids_v, sem, in_sem, out_sem):
    del c_in, term_in
    ins = fetch(((part_h, part), (ra_h.at[:, block(0)], ra), (tpt_h, tpt)), in_sem)
    read_meta([(m2, ROW_META), (m1, TAIL_META), (own, TAIL_META)], meta_v, meta_s, sem)
    write_ids(tbuf, 1, ids_v, meta_v, (2, 2, 1))
    smooth_far(m2, flat, smm, meta_s, 0, inside(slab, -2, slabs))
    place_q(qs, m1, TAIL_Q, meta_s, 1, inside(slab, -1, slabs))
    for copy in ins:
        copy.wait()
    pw[...] = (part[...] - dot(ra[...], smm[:, block(2)])).astype(BF16)
    cbuf[...] = dot(pw[...], qs[...])
    out = pltpu.make_async_copy(cbuf, c_ref.at[:, block(2)], out_sem.at[0])
    out.start()
    write_term(tbuf, 0, tpt, cbuf[...], m1, TAIL_T)
    sent = pltpu.make_async_copy(tbuf, term_ref.at[:, W:], out_sem.at[1])
    sent.start()
    smm_out[...] = smm[:, 0:2 * W]
    out.wait()
    sent.wait()


def second(slab, m2, m1, own, part, ra, tpt, c, term):
    shape = jax.ShapeDtypeStruct
    return pl.pallas_call(
        functools.partial(second_kernel, lax.axis_size("slab")),
        out_shape=(shape((W, 7 * W), F32), shape((W, 2 * W + LANES), BF16), shape((W, 2 * W), BF16)),
        grid=(1,),
        in_specs=[SMEM, VMEM, TAIL, TAIL] + [ANY] * 5,
        out_specs=(ANY, ANY, VMEM),
        input_output_aliases={7: 0, 8: 1},
        scratch_shapes=[
            pltpu.VMEM((W, W), BF16),
            pltpu.VMEM((W, WIDE), BF16),
            pltpu.VMEM((W, W), BF16),
            pltpu.VMEM((W, W), BF16),
            pltpu.VMEM((W, W), F32),
            pltpu.VMEM((W, W), BF16),
            pltpu.VMEM((W, W), BF16),
            pltpu.VMEM((W, W), F32),
            pltpu.VMEM((W, W + LANES), BF16),
            pltpu.VMEM((3, 16, LANES), I32),
            pltpu.SMEM((3, 16, LANES), I32),
            pltpu.VMEM((CHUNK, LANES), F32),
            pltpu.SemaphoreType.DMA((3,)),
            pltpu.SemaphoreType.DMA((3,)),
            pltpu.SemaphoreType.DMA((2,)),
        ],
        compiler_params=params(),
        cost_estimate=pl.CostEstimate(flops=4_000_000_000, bytes_accessed=8 << 20, transcendentals=0),
    )(slab, m2, m1, own, part, ra, tpt, c, term)


def write_columns(slab, slabs, qs, pw, cbuf, c_ref, out_sem, tpt, meta_s, outs, term, n, value, o, ref, top, at):
    pw[...] = value.astype(BF16)
    place_q(qs, ref, top, meta_s, at, inside(slab, o - 3, slabs))
    cbuf[n] = dot(pw[...], qs[...])
    outs.append(pltpu.make_async_copy(cbuf.at[n], c_ref.at[:, block(o)], out_sem.at[n]))
    outs[-1].start()
    write_term(term, n, tpt, cbuf[n], ref, top + TILE)


def third_kernel(slabs, slab, p2, p1, m2, sm_h, smm_h, smo_h, ra_h, tpt_h, c_in, c_ref, term_ref, smp_h,
                 flat, smp, qs, pw, cbuf, tbuf, sm1, smm, smo, ra, tpt, meta_v, meta_s, sem, in_sem, out_sem):
    del c_in
    ins = fetch(((sm_h.at[:, block(2)], sm1), (smm_h.at[:, block(1)], smm), (smo_h, smo), (ra_h, ra), (tpt_h, tpt)), in_sem)
    read_meta([(p2, ROW_META), (p1, TAIL_META), (m2, TAIL_META)], meta_v, meta_s, sem)
    smooth_far(p2, flat, smp, meta_s, 0, inside(slab, 2, slabs))
    for copy in ins:
        copy.wait()
    outs = [pltpu.make_async_copy(smp.at[:, block(2)], smp_h, out_sem.at[3])]
    outs[0].start()
    columns = functools.partial(write_columns, slab, slabs, qs, pw, cbuf, c_ref, out_sem, tpt, meta_s, outs, tbuf)
    first, last, beside = ra[:, block(0)], ra[:, block(4)], ra[:, block(3)]
    value = beside.astype(F32) - dot(beside, smo[:, block(1)]) - dot(ra[:, block(2)], sm1[...])
    columns(0, value - dot(last, smp[:, block(0)]), 4, p1, TAIL_Q, 1)
    value = first.astype(F32) - dot(first, smm[...]) - dot(ra[:, block(1)], smo[:, block(0)])
    columns(1, value, 1, m2, TAIL_Q, 2)
    value = last.astype(F32) - dot(last, smp[:, block(1)]) - dot(beside, smo[:, block(2)])
    columns(2, value, 5, p2, ROW_Q, 0)
    outs.append(pltpu.make_async_copy(tbuf, term_ref.at[:, 0:3 * W], out_sem.at[4]))
    outs[-1].start()
    for out in outs:
        out.wait()


def third(slab, p2, p1, m2, sm, smm, smo, ra, tpt, c):
    shape = jax.ShapeDtypeStruct
    return pl.pallas_call(
        functools.partial(third_kernel, lax.axis_size("slab")),
        out_shape=(shape((W, 7 * W), F32), shape((W, 5 * W + LANES), BF16), shape((W, W), BF16)),
        grid=(1,),
        in_specs=[SMEM, VMEM, TAIL, TAIL] + [ANY] * 6,
        out_specs=(ANY, ANY, ANY),
        input_output_aliases={9: 0},
        scratch_shapes=[
            pltpu.VMEM((W, W), BF16),
            pltpu.VMEM((W, WIDE), BF16),
            pltpu.VMEM((W, W), BF16),
            pltpu.VMEM((W, W), BF16),
            pltpu.VMEM((3, W, W), F32),
            pltpu.VMEM((W, 3 * W), BF16),
            pltpu.VMEM((W, W), BF16),
            pltpu.VMEM((W, W), BF16),
            pltpu.VMEM((W, 3 * W), BF16),
            pltpu.VMEM((W, 5 * W), BF16),
            pltpu.VMEM((W, W), BF16),
            pltpu.VMEM((3, 16, LANES), I32),
            pltpu.SMEM((3, 16, LANES), I32),
            pltpu.SemaphoreType.DMA((3,)),
            pltpu.SemaphoreType.DMA((5,)),
            pltpu.SemaphoreType.DMA((5,)),
        ],
        compiler_params=params(),
        cost_estimate=pl.CostEstimate(flops=6_000_000_000, bytes_accessed=12 << 20, transcendentals=0),
    )(slab, p2, p1, m2, sm, smm, smo, ra, tpt, c)


def fourth_kernel(slabs, slab, m3, p3, p2, p1, m2, own, smm_h, smp_h, ra_h, tpt_h, c_in, term_in, c_ref, term_ref,
                  qs, pw, cbuf, tbuf, smm, smp, ra0, ra4, tpt, meta_v, meta_s, ids_v, sem, in_sem, out_sem):
    del c_in, term_in
    ins = fetch(((smm_h.at[:, block(0)], smm), (smp_h, smp), (ra_h.at[:, block(0)], ra0),
                 (ra_h.at[:, block(4)], ra4), (tpt_h, tpt)), in_sem)
    read_meta([(ref, TAIL_META) for ref in (p2, p1, m2, m3, p3, own)], meta_v, meta_s, sem)
    write_ids(tbuf, 2, ids_v, meta_v, (5, 1, 2, 0, 3, 4))
    for copy in ins:
        copy.wait()
    outs = []
    columns = functools.partial(write_columns, slab, slabs, qs, pw, cbuf, c_ref, out_sem, tpt, meta_s, outs, tbuf)
    columns(0, -dot(ra0[...], smm[...]), 0, m3, TAIL_Q, 3)
    columns(1, -dot(ra4[...], smp[...]), 6, p3, TAIL_Q, 4)
    outs.append(pltpu.make_async_copy(tbuf, term_ref.at[:, 3 * W:], out_sem.at[2]))
    outs[-1].start()
    for out in outs:
        out.wait()


def fourth(slab, m3, p3, p2, p1, m2, own, smm, smp, ra, tpt, c, term):
    shape = jax.ShapeDtypeStruct
    return pl.pallas_call(
        functools.partial(fourth_kernel, lax.axis_size("slab")),
        out_shape=(shape((W, 7 * W), F32), shape((W, 5 * W + LANES), BF16)),
        grid=(1,),
        in_specs=[SMEM, VMEM, VMEM] + [TAIL] * 4 + [ANY] * 6,
        out_specs=(ANY, ANY),
        input_output_aliases={11: 0, 12: 1},
        scratch_shapes=[pltpu.VMEM((W, W), BF16)] * 2
        + [pltpu.VMEM((2, W, W), F32), pltpu.VMEM((W, 2 * W + LANES), BF16)]
        + [pltpu.VMEM((W, W), BF16)] * 5
        + [
            pltpu.VMEM((6, 16, LANES), I32),
            pltpu.SMEM((6, 16, LANES), I32),
            pltpu.VMEM((CHUNK, LANES), F32),
            pltpu.SemaphoreType.DMA((6,)),
            pltpu.SemaphoreType.DMA((5,)),
            pltpu.SemaphoreType.DMA((3,)),
        ],
        compiler_params=params(),
        cost_estimate=pl.CostEstimate(flops=3_000_000_000, bytes_accessed=8 << 20, transcendentals=0),
    )(slab, m3, p3, p2, p1, m2, own, smm, smp, ra, tpt, c, term)


def gather_pieces(count, x_ref, lows, highs, ids_v, ids_s, sem):
    for p in range(GROUPS):
        ids_v[p] = x_ref[p, 0:8, count * W:].astype(F32).astype(I32)
    to_scalars([(ids_v, ids_s)], sem)
    for y in lows + highs:
        y[...] = jnp.zeros_like(y)

    def one(p, carry):
        rows = pl.ds(pl.multiple_of(p * CHUNK, CHUNK), CHUNK)
        for w in range(N // 2):
            sides = [
                [halves(x_ref[p + d, :, o * W + w * LANES:o * W + (w + 1) * LANES]) for d in (0, GROUPS // 2)]
                for o in range(count)
            ]
            for h in range(2):
                for o in range(count):
                    for y, side, d in ((lows[o], sides[o][0], 0), (highs[o], sides[o][1], GROUPS // 2)):
                        g = ids_s[p + d, 1 + o, 2 * w + h]
                        y[rows, window(g)] = y[rows, window(g)] + pick(side[h], g)
        return carry

    lax.fori_loop(0, GROUPS // 2, one, 0)


def add_pieces(count, first, takes, lows, highs, out_ref):
    for o in range(count):
        total = None
        for cq in range(4):
            cols = slice(cq * QUARTER, (cq + 1) * QUARTER)
            piece = dot(takes[cq, :, 0:256], lows[o][:, cols]) + dot(takes[cq, :, 256:W], highs[o][:, cols])
            total = piece if total is None else total + piece
        out_ref[:, (first + o) * QUARTER:(first + o + 1) * QUARTER] = total.astype(BF16)


def merge_first_kernel(count, x_ref, out_ref, takes, *rest):
    lows, highs, (ids_v, ids_s, sem) = rest[:count], rest[count:2 * count], rest[2 * count:]
    gather_pieces(count, x_ref, lows, highs, ids_v, ids_s, sem)
    groups = jnp.concatenate([ids_v[p, 0:1, :] for p in range(GROUPS)], axis=0).astype(F32).astype(BF16)
    spread = (((iota((LANES, W), 1) >> 2) & 7) == iota((LANES, W), 0)).astype(F32).astype(BF16)
    each = dot(groups, spread)
    mine = (iota((GROUPS, W), 1) >> 5) == iota((GROUPS, W), 0)
    group = jnp.sum(jnp.where(mine, each, 0.0), axis=0, keepdims=True).astype(I32)
    row, col = iota((256, W), 0), iota((256, W), 1)
    hit = ((row >> 4) == group) & ((row & 3) == (col & 3))
    for cq in range(4):
        takes[cq] = (hit & (((row >> 2) & 3) == cq)).astype(F32).astype(BF16)
    add_pieces(count, 0, takes, lows, highs, out_ref)


def merge_last_kernel(count, x_ref, done, takes, out_ref, *rest):
    lows, highs, (ids_v, ids_s, sem) = rest[:count], rest[count:2 * count], rest[2 * count:]
    out_ref[:, 0:done.shape[1]] = done[...]
    gather_pieces(count, x_ref, lows, highs, ids_v, ids_s, sem)
    add_pieces(count, done.shape[1] // QUARTER, takes, lows, highs, out_ref)


def merge(x, done=None, takes=None):
    count = x.shape[2] // W
    shape = jax.ShapeDtypeStruct
    first = done is None
    earlier = 0 if first else done.shape[1] // QUARTER
    out = shape((256, (earlier + count) * QUARTER), BF16)
    return pl.pallas_call(
        functools.partial(merge_first_kernel if first else merge_last_kernel, count),
        out_shape=(out, shape((4, 256, W), BF16)) if first else out,
        in_specs=[VMEM] * (1 if first else 3),
        out_specs=(VMEM, VMEM) if first else VMEM,
        scratch_shapes=[pltpu.VMEM((GROUPS * CHUNK // 2, GROUPS * TILE), BF16)] * (2 * count)
        + [
            pltpu.VMEM((GROUPS, 8, LANES), I32),
            pltpu.SMEM((GROUPS, 8, LANES), I32),
            pltpu.SemaphoreType.DMA((1,)),
        ],
        compiler_params=params(),
        cost_estimate=pl.CostEstimate(flops=1_000_000_000 * count, bytes_accessed=count << 20, transcendentals=0),
    )(*((x,) if first else (x, done, takes)))


def finish_kernel(order, x_ref, out_h, out_ref, sem):
    row, col = iota((TILE, 256), 0), iota((TILE, 256), 1)
    same = ((row >> 2) == (col >> 4)) & ((row & 3) == (col & 3))
    takes = [(same & (((col >> 2) & 3) == cq)).astype(F32).astype(BF16) for cq in range(4)]
    copies = []
    for n, o in enumerate(order):
        for cq in range(4):
            at = o * 4 * QUARTER + cq * QUARTER
            out_ref[0, :, at:at + QUARTER] = dot(takes[cq], x_ref[:, n * QUARTER:(n + 1) * QUARTER])
        cols = slice(o * 4 * QUARTER, (o + 1) * 4 * QUARTER)
        copies.append(pltpu.make_async_copy(out_ref.at[:, :, cols], out_h.at[:, :, cols], sem.at[n]))
        copies[n].start()
    for copy in copies:
        copy.wait()


def finish(order, x):
    shape = (1, TILE, DENSE)
    return pl.pallas_call(
        functools.partial(finish_kernel, order),
        out_shape=jax.ShapeDtypeStruct(shape, F32),
        in_specs=[VMEM],
        out_specs=ANY,
        scratch_shapes=[pltpu.VMEM(shape, F32), pltpu.SemaphoreType.DMA((len(order),))],
        compiler_params=params(),
    )(x)


def along(block, step):
    count = lax.axis_size("slab")
    route = [(i, (i + step) % count) for i in range(count)]
    return lax.ppermute(block, "slab", route)


def exchange(term):
    return lax.all_to_all(term.reshape(GROUPS, CHUNK, term.shape[1]), "piece", 0, 0)


def hand_over(dense):
    back = lax.all_to_all(dense.reshape(GROUPS, 16, dense.shape[1]), "piece", 0, 0)
    return back.reshape(256, dense.shape[1])


def device_part(fine_tiles, fine_cols, bond_mask, diag_inv, tentative, aggregate, tentative_two, aggregate_two):
    own = pack(fine_tiles, diag_inv, tentative, tentative_two, fine_cols, bond_mask, aggregate, aggregate_two)
    m1, p1 = along(own, 1), along(own, -1)
    slab = lax.axis_index("slab").astype(I32).reshape(1)
    rap, sm, qs, r0, tpt = start_own(own)
    m2 = along(m1, 1)
    p2 = along(p1, -1)
    c, term, part, ra, smo, m1_tail, p1_tail = near(slab, m1, p1, rap, sm, qs, r0, tpt, own)
    m3 = along(m1_tail, 2)
    p3 = along(p1_tail, -2)
    c, term, smm = second(slab, m2, m1, own, part, ra, tpt, c, term)
    got = exchange(term)
    c, term, smp = third(slab, p2, p1, m2, sm, smm, smo, ra, tpt, c)
    c, term = fourth(slab, m3, p3, p2, p1, m2, own, smm, smp, ra, tpt, c, term)
    last = exchange(term)
    done, takes = merge(got)
    level_two = finish((3, 2, 4, 1, 5, 0, 6), hand_over(merge(last, done, takes)))
    return c.reshape(N, TILE, 7 * W), level_two


def solution(mesh):
    both = ("slab", "piece")
    placed = (
        P(both, None, None), P(both, None), P(both, None), P(both, None, None),
        P(both, None, None), P(both), P(both, None, None), P(both),
    )
    return jax.shard_map(
        device_part,
        mesh=mesh,
        in_specs=placed,
        out_specs=(P(both, None, None), P(both, None, None)),
        check_vma=False,
    )
```

```python
import functools

import jax
import jax.numpy as jnp
from jax import lax
from jax.experimental import pallas as pl
from jax.experimental.pallas import tpu as pltpu
from jax.sharding import PartitionSpec as P


DAMPING = 2.0 / 3.0
TILE = 64
N = 8
W = N * TILE
LANES = 128
TRASH = 3 * N
WIDE = 3 * W + LANES
ROW_D, ROW_Q, ROW_T, ROW_META, ROWS = W, W + 64, W + 128, W + 192, W + 208
ANY = pl.BlockSpec(memory_space=pl.ANY)
VMEM = pl.BlockSpec(memory_space=pltpu.VMEM)
SMEM = pl.BlockSpec(memory_space=pltpu.SMEM)
BF16, F32, I32 = jnp.bfloat16, jnp.float32, jnp.int32
GROUPS = 16
PART = 4
CHUNK = N * PART
DENSE = 7 * GROUPS * TILE
QUARTER = GROUPS * TILE // 4
TAIL = pl.BlockSpec((144, W), lambda i: (ROW_Q // 144, 0))
TAIL_Q, TAIL_T, TAIL_META = 0, 64, 128


def params():
    return pltpu.CompilerParams(vmem_limit_bytes=67_043_328)


def dot(a, b):
    return jnp.dot(a, b, preferred_element_type=F32)


def iota(shape, dim):
    return lax.broadcasted_iota(I32, shape, dim)


def pack_kernel(a_ref, d_ref, q_ref, t_ref, cols_ref, mask_ref, agg_ref, agg2_ref, out_ref, meta):
    for i in range(N):
        out_ref[i * TILE:(i + 1) * TILE, :] = a_ref[i]
    for row, ref in ((ROW_D, d_ref), (ROW_Q, q_ref), (ROW_T, t_ref)):
        for w in range(N // 2):
            pair = jnp.concatenate([ref[2 * w], ref[2 * w + 1]], axis=1)
            out_ref[row:row + TILE, w * LANES:(w + 1) * LANES] = pair
    meta[...] = jnp.zeros_like(meta)
    meta[0:8, 0:8] = jnp.where(mask_ref[...] > 0, cols_ref[...], TRASH).astype(F32)
    meta[8:9, 0:8] = agg_ref[...].astype(F32)
    meta[9:10, 0:8] = agg2_ref[...].astype(F32)
    out_ref[ROW_META:ROWS, :] = meta[...].astype(BF16)


def pack(a, d, q, t, cols, mask, agg, agg2):
    return pl.pallas_call(
        pack_kernel,
        out_shape=jax.ShapeDtypeStruct((ROWS, W), BF16),
        in_specs=[VMEM] * 8,
        out_specs=VMEM,
        scratch_shapes=[pltpu.VMEM((16, W), F32)],
        compiler_params=params(),
    )(a, d, q, t, cols, mask, agg.reshape(1, N), agg2.reshape(1, N))


def halves(x):
    high = iota(x.shape, 1) >= TILE
    swapped = jnp.concatenate([x[:, TILE:], x[:, :TILE]], axis=1)
    zero = jnp.zeros_like(x)
    return (
        (jnp.where(high, zero, x), jnp.where(high, swapped, zero)),
        (jnp.where(high, zero, swapped), jnp.where(high, x, zero)),
    )


def window(index):
    return pl.ds(pl.multiple_of((index >> 1) * LANES, LANES), LANES)


def pick(variants, index):
    return jnp.where((index & 1) == 1, variants[1], variants[0])


def block_diagonal(row):
    block = iota(row.shape, 1) // TILE
    zero = jnp.zeros_like(row)
    return jnp.concatenate([jnp.where(block == i, row, zero) for i in range(N)], axis=0)


def to_scalars(pairs, sem):
    copies = [pltpu.make_async_copy(v, s, sem.at[n]) for n, (v, s) in enumerate(pairs)]
    for c in copies:
        c.start()
    for c in copies:
        c.wait()


def read_meta(tails, meta_v, meta_s, sem):
    for n, (ref, top) in enumerate(tails):
        meta_v[n] = ref[top:top + 16, 0:LANES].astype(F32).astype(I32)
    to_scalars([(meta_v.at[n], meta_s.at[n]) for n in range(len(tails))], sem)


def inside(slab, step, slabs):
    at = slab[0] + step
    return (at >= 0) & (at < slabs)


def place_q(out, ref, top, meta_s, n, valid=None):
    out[...] = jnp.zeros((W, W), BF16)
    for w in range(N // 2):
        sides = halves(ref[top:top + TILE, w * LANES:(w + 1) * LANES])
        for h in range(2):
            c = 2 * w + h
            g = meta_s[n, 8, c]
            out[c * TILE:(c + 1) * TILE, window(g)] = pick(sides[h], g)
    if valid is not None:
        @pl.when(jnp.logical_not(valid))
        def _():
            out[...] = jnp.zeros((W, W), BF16)


def pair_diagonal(pair):
    high = iota(pair.shape, 1) >= TILE
    zero = jnp.zeros_like(pair)
    return jnp.concatenate([jnp.where(high, zero, pair), jnp.where(high, pair, zero)], axis=0)


def place_a(refs, outs, sms, meta_s, metas, valids=None):
    def place_row(i, carry):
        rows = pl.ds(pl.multiple_of(i * TILE, TILE), TILE)
        for out in outs:
            out[rows, :] = jnp.zeros((TILE, WIDE), BF16)
        for w in range(N // 2):
            sides = [halves(ref[rows, w * LANES:(w + 1) * LANES]) for ref in refs]
            for h in range(2):
                for out, side, n in zip(outs, sides, metas):
                    c = meta_s[n, i, 2 * w + h]
                    if valids is not None:
                        c = jnp.where(valids[n], c, TRASH)
                    out[rows, window(c)] = out[rows, window(c)] + pick(side[h], c)
        return carry

    lax.fori_loop(0, N, place_row, 0)

    def smooth(w, carry):
        rows = pl.ds(pl.multiple_of(w * LANES, LANES), LANES)
        for ref, out, sm in zip(refs, outs, sms):
            diag = pair_diagonal(ref[ROW_D:ROW_D + TILE, rows])
            sm[rows, :] = (DAMPING * dot(diag, out[rows, 0:3 * W])).astype(BF16)
        return carry

    lax.fori_loop(0, N // 2, smooth, 0)


def write_term(term, n, tpt, c, ref, top):
    lhs = dot(tpt[...], c.astype(BF16)).astype(BF16)
    for w in range(N // 2):
        diag = pair_diagonal(ref[top:top + TILE, w * LANES:(w + 1) * LANES])
        at = n * W + w * LANES
        term[:, at:at + LANES] = dot(lhs[:, w * LANES:(w + 1) * LANES], diag).astype(BF16)


def write_ids(term, count, ids_v, meta_v, order):
    ids_v[...] = jnp.zeros_like(ids_v)
    for row, n in enumerate(order):
        ids_v[row:row + 1, :] = meta_v[n, 9:10, :].astype(F32)
    for q in range(GROUPS):
        term[q * CHUNK:(q + 1) * CHUNK, count * W:] = ids_v[...].astype(BF16)


def block(j):
    return slice(j * W, (j + 1) * W)


def own_kernel(own, rap, sm, qs, r0, tpt, ad, meta_v, meta_s, sem):
    read_meta([(own, ROW_META)], meta_v, meta_s, sem)
    place_q(qs, own, ROW_Q, meta_s, 0)
    place_a((own,), (ad,), (sm,), meta_s, (0,))
    r0[...] = (qs[...].astype(F32) - dot(sm[:, block(1)], qs[...])).astype(BF16)
    turned = r0[...].T
    for j in range(3):
        rap[:, block(j)] = dot(turned, ad[:, block(j)])
    left = block_diagonal(own[ROW_T:ROW_T + TILE, :])
    lead = iota((W, W), 0)
    target = ((lead >> 2) & 7) * TILE + (lead >> 5) * PART + (lead & 3)
    turn = (target == iota((W, W), 1)).astype(F32).astype(BF16)
    tpt[...] = lax.dot_general(turn, left, (((1,), (1,)), ((), ())), preferred_element_type=F32).astype(BF16)


def start_own(own):
    shape = jax.ShapeDtypeStruct
    return pl.pallas_call(
        own_kernel,
        out_shape=(
            shape((W, 3 * W), F32), shape((W, 3 * W), BF16), shape((W, W), BF16),
            shape((W, W), BF16), shape((W, W), BF16),
        ),
        in_specs=[VMEM],
        out_specs=(VMEM,) * 5,
        scratch_shapes=[
            pltpu.VMEM((W, WIDE), BF16),
            pltpu.VMEM((1, 16, LANES), I32),
            pltpu.SMEM((1, 16, LANES), I32),
            pltpu.SemaphoreType.DMA((1,)),
        ],
        compiler_params=params(),
        cost_estimate=pl.CostEstimate(flops=3_000_000_000, bytes_accessed=6 << 20, transcendentals=0),
    )(own)


def fetch(pairs, sem):
    copies = [pltpu.make_async_copy(src, dst, sem.at[n]) for n, (src, dst) in enumerate(pairs)]
    for c in copies:
        c.start()
    return copies


def near_kernel(slabs, slab, m1, p1, rap_h, sm_h, qs_h, r0_h, tpt_h, own,
                c_ref, term_ref, part_h, ra_h, smo_h, m1_tail, p1_tail,
                ad0, ad2, sm0, sm1, sm2, qs1, rm, r0, rp, tpt, rap, ra, part, cbuf, tbuf,
                meta_v, meta_s, sem, in_sem, out_sem):
    ins = fetch(((qs_h, qs1), (rap_h, rap), (r0_h, r0), (tpt_h, tpt), (sm_h, sm1)), in_sem)
    outs = []

    def send(src, dst):
        outs.append(pltpu.make_async_copy(src, dst, out_sem.at[len(outs)]))
        outs[-1].start()

    send(m1.at[ROW_Q:ROWS, :], m1_tail)
    send(p1.at[ROW_Q:ROWS, :], p1_tail)
    read_meta([(m1, ROW_META), (p1, ROW_META)], meta_v, meta_s, sem)
    valids = (inside(slab, -1, slabs), inside(slab, 1, slabs))
    place_a((m1, p1), (ad0, ad2), (sm0, sm2), meta_s, (0, 1), valids)
    send(sm0.at[:, block(0)], smo_h.at[:, block(0)])
    send(sm2.at[:, W:3 * W], smo_h.at[:, W:3 * W])
    for copy in ins:
        copy.wait()

    rm[...] = (-dot(sm0[:, block(2)], qs1[...])).astype(BF16)
    rp[...] = (-dot(sm2[:, block(0)], qs1[...])).astype(BF16)
    before, after = rm[...].T, rp[...].T
    ra[:, block(0)] = dot(before, ad0[:, block(0)]).astype(BF16)
    ra[:, block(1)] = (dot(before, ad0[:, block(1)]) + rap[:, block(0)]).astype(BF16)
    ra[:, block(2)] = (dot(before, ad0[:, block(2)]) + dot(after, ad2[:, block(0)]) + rap[:, block(1)]).astype(BF16)
    ra[:, block(3)] = (dot(after, ad2[:, block(1)]) + rap[:, block(2)]).astype(BF16)
    ra[:, block(4)] = dot(after, ad2[:, block(2)]).astype(BF16)
    send(ra, ra_h)

    lead = ra[:, block(1)]
    part[...] = lead.astype(F32) - dot(lead, sm0[:, block(1)]) - dot(ra[:, block(2)], sm1[:, block(0)])
    send(part, part_h)
    cbuf[...] = dot(ra[:, block(1)], rm[...]) + dot(ra[:, block(2)], r0[...]) + dot(ra[:, block(3)], rp[...])
    send(cbuf, c_ref.at[:, block(3)])
    write_term(tbuf, 0, tpt, cbuf[...], own, TAIL_T)
    send(tbuf, term_ref.at[:, block(0)])
    for copy in outs:
        copy.wait()


def near(slab, m1, p1, rap, sm, qs, r0, tpt, own):
    shape = jax.ShapeDtypeStruct
    return pl.pallas_call(
        functools.partial(near_kernel, lax.axis_size("slab")),
        grid=(1,),
        out_shape=(
            shape((W, 7 * W), F32), shape((W, 2 * W + LANES), BF16), shape((W, W), F32),
            shape((W, 5 * W), BF16), shape((W, 3 * W), BF16), shape((144, W), BF16), shape((144, W), BF16),
        ),
        in_specs=[SMEM, VMEM, VMEM] + [ANY] * 5 + [TAIL],
        out_specs=(ANY,) * 7,
        scratch_shapes=[pltpu.VMEM((W, WIDE), BF16)] * 2
        + [pltpu.VMEM((W, 3 * W), BF16)] * 3
        + [pltpu.VMEM((W, W), BF16)] * 5
        + [
            pltpu.VMEM((W, 3 * W), F32),
            pltpu.VMEM((W, 5 * W), BF16),
            pltpu.VMEM((W, W), F32),
            pltpu.VMEM((W, W), F32),
            pltpu.VMEM((W, W), BF16),
            pltpu.VMEM((2, 16, LANES), I32),
            pltpu.SMEM((2, 16, LANES), I32),
            pltpu.SemaphoreType.DMA((2,)),
            pltpu.SemaphoreType.DMA((5,)),
            pltpu.SemaphoreType.DMA((8,)),
        ],
        compiler_params=params(),
        cost_estimate=pl.CostEstimate(flops=9_000_000_000, bytes_accessed=14 << 20, transcendentals=0),
    )(slab, m1, p1, rap, sm, qs, r0, tpt, own)


def smooth_far(ref, flat, sm, meta_s, n, valid):
    for w in range(N // 2):
        rows = slice(w * LANES, (w + 1) * LANES)
        diag = pair_diagonal(ref[ROW_D:ROW_D + TILE, rows])
        flat[rows, :] = (DAMPING * dot(diag, ref[rows, :])).astype(BF16)
    tops = (0, W // 2)

    def place_row(i, carry):
        starts = [pl.ds(pl.multiple_of(top + i * TILE, TILE), TILE) for top in tops]
        for rows in starts:
            sm[rows, :] = jnp.zeros((TILE, WIDE), BF16)
        for w in range(N // 2):
            sides = [halves(flat[rows, w * LANES:(w + 1) * LANES]) for rows in starts]
            for h in range(2):
                for d, rows in enumerate(starts):
                    c = jnp.where(valid, meta_s[n, i + d * N // 2, 2 * w + h], TRASH)
                    sm[rows, window(c)] = sm[rows, window(c)] + pick(sides[d][h], c)
        return carry

    lax.fori_loop(0, N // 2, place_row, 0)


def second_kernel(slabs, slab, m2, m1, own, part_h, ra_h, tpt_h, c_in, term_in, c_ref, term_ref, smm_out,
                  flat, smm, qs, pw, part, ra, tpt, cbuf, tbuf, meta_v, meta_s, ids_v, sem, in_sem, out_sem):
    del c_in, term_in
    ins = fetch(((part_h, part), (ra_h.at[:, block(0)], ra), (tpt_h, tpt)), in_sem)
    read_meta([(m2, ROW_META), (m1, TAIL_META), (own, TAIL_META)], meta_v, meta_s, sem)
    write_ids(tbuf, 1, ids_v, meta_v, (2, 2, 1))
    smooth_far(m2, flat, smm, meta_s, 0, inside(slab, -2, slabs))
    place_q(qs, m1, TAIL_Q, meta_s, 1, inside(slab, -1, slabs))
    for copy in ins:
        copy.wait()
    pw[...] = (part[...] - dot(ra[...], smm[:, block(2)])).astype(BF16)
    cbuf[...] = dot(pw[...], qs[...])
    out = pltpu.make_async_copy(cbuf, c_ref.at[:, block(2)], out_sem.at[0])
    out.start()
    write_term(tbuf, 0, tpt, cbuf[...], m1, TAIL_T)
    sent = pltpu.make_async_copy(tbuf, term_ref.at[:, W:], out_sem.at[1])
    sent.start()
    smm_out[...] = smm[:, 0:2 * W]
    out.wait()
    sent.wait()


def second(slab, m2, m1, own, part, ra, tpt, c, term):
    shape = jax.ShapeDtypeStruct
    return pl.pallas_call(
        functools.partial(second_kernel, lax.axis_size("slab")),
        out_shape=(shape((W, 7 * W), F32), shape((W, 2 * W + LANES), BF16), shape((W, 2 * W), BF16)),
        grid=(1,),
        in_specs=[SMEM, VMEM, TAIL, TAIL] + [ANY] * 5,
        out_specs=(ANY, ANY, VMEM),
        input_output_aliases={7: 0, 8: 1},
        scratch_shapes=[
            pltpu.VMEM((W, W), BF16),
            pltpu.VMEM((W, WIDE), BF16),
            pltpu.VMEM((W, W), BF16),
            pltpu.VMEM((W, W), BF16),
            pltpu.VMEM((W, W), F32),
            pltpu.VMEM((W, W), BF16),
            pltpu.VMEM((W, W), BF16),
            pltpu.VMEM((W, W), F32),
            pltpu.VMEM((W, W + LANES), BF16),
            pltpu.VMEM((3, 16, LANES), I32),
            pltpu.SMEM((3, 16, LANES), I32),
            pltpu.VMEM((CHUNK, LANES), F32),
            pltpu.SemaphoreType.DMA((3,)),
            pltpu.SemaphoreType.DMA((3,)),
            pltpu.SemaphoreType.DMA((2,)),
        ],
        compiler_params=params(),
        cost_estimate=pl.CostEstimate(flops=4_000_000_000, bytes_accessed=8 << 20, transcendentals=0),
    )(slab, m2, m1, own, part, ra, tpt, c, term)


def third_kernel(slabs, slab, p2, p1, m3, m2, p3, own, sm_h, smm_h, smo_h, ra_h, tpt_h, c_in, c_ref, term,
                 flat, smp, qs, pw, cbuf, sm1, smm, smo, ra, tpt, meta_v, meta_s, ids_v, sem, in_sem, out_sem):
    del c_in
    ins = fetch(((sm_h.at[:, block(2)], sm1), (smm_h, smm), (smo_h, smo), (ra_h, ra), (tpt_h, tpt)), in_sem)
    read_meta([(p2, ROW_META)] + [(ref, TAIL_META) for ref in (p1, m2, m3, p3, own)], meta_v, meta_s, sem)
    write_ids(term, 5, ids_v, meta_v, (5, 1, 2, 0, 3, 4))
    smooth_far(p2, flat, smp, meta_s, 0, inside(slab, 2, slabs))
    for copy in ins:
        copy.wait()
    outs = []

    def columns(n, value, o, ref, top, at):
        pw[...] = value.astype(BF16)
        place_q(qs, ref, top, meta_s, at, inside(slab, o - 3, slabs))
        cbuf[n] = dot(pw[...], qs[...])
        outs.append(pltpu.make_async_copy(cbuf.at[n], c_ref.at[:, block(o)], out_sem.at[n]))
        outs[-1].start()
        write_term(term, n, tpt, cbuf[n], ref, top + TILE)

    first, last = ra[:, block(0)], ra[:, block(4)]
    near = ra[:, block(3)]
    value = near.astype(F32) - dot(near, smo[:, block(1)]) - dot(ra[:, block(2)], sm1[...])
    columns(0, value - dot(last, smp[:, block(0)]), 4, p1, TAIL_Q, 1)
    value = first.astype(F32) - dot(first, smm[:, block(1)]) - dot(ra[:, block(1)], smo[:, block(0)])
    columns(1, value, 1, m2, TAIL_Q, 2)
    value = last.astype(F32) - dot(last, smp[:, block(1)]) - dot(near, smo[:, block(2)])
    columns(2, value, 5, p2, ROW_Q, 0)
    columns(3, -dot(first, smm[:, block(0)]), 0, m3, TAIL_Q, 3)
    columns(4, -dot(last, smp[:, block(2)]), 6, p3, TAIL_Q, 4)
    for out in outs:
        out.wait()


def third(slab, p2, p1, m3, m2, p3, own, sm, smm, smo, ra, tpt, c):
    shape = jax.ShapeDtypeStruct
    return pl.pallas_call(
        functools.partial(third_kernel, lax.axis_size("slab")),
        out_shape=(shape((W, 7 * W), F32), shape((W, 5 * W + LANES), BF16)),
        grid=(1,),
        in_specs=[SMEM, VMEM, TAIL, VMEM, TAIL, VMEM, TAIL] + [ANY] * 6,
        out_specs=(ANY, VMEM),
        input_output_aliases={12: 0},
        scratch_shapes=[
            pltpu.VMEM((W, W), BF16),
            pltpu.VMEM((W, WIDE), BF16),
            pltpu.VMEM((W, W), BF16),
            pltpu.VMEM((W, W), BF16),
            pltpu.VMEM((5, W, W), F32),
            pltpu.VMEM((W, W), BF16),
            pltpu.VMEM((W, 2 * W), BF16),
            pltpu.VMEM((W, 3 * W), BF16),
            pltpu.VMEM((W, 5 * W), BF16),
            pltpu.VMEM((W, W), BF16),
            pltpu.VMEM((6, 16, LANES), I32),
            pltpu.SMEM((6, 16, LANES), I32),
            pltpu.VMEM((CHUNK, LANES), F32),
            pltpu.SemaphoreType.DMA((6,)),
            pltpu.SemaphoreType.DMA((5,)),
            pltpu.SemaphoreType.DMA((5,)),
        ],
        compiler_params=params(),
        cost_estimate=pl.CostEstimate(flops=7_000_000_000, bytes_accessed=18 << 20, transcendentals=0),
    )(slab, p2, p1, m3, m2, p3, own, sm, smm, smo, ra, tpt, c)


def gather_pieces(count, x_ref, lows, highs, ids_v, ids_s, sem):
    for p in range(GROUPS):
        ids_v[p] = x_ref[p, 0:8, count * W:].astype(F32).astype(I32)
    to_scalars([(ids_v, ids_s)], sem)
    for y in lows + highs:
        y[...] = jnp.zeros_like(y)

    def one(p, carry):
        rows = pl.ds(pl.multiple_of(p * CHUNK, CHUNK), CHUNK)
        for w in range(N // 2):
            sides = [
                [halves(x_ref[p + d, :, o * W + w * LANES:o * W + (w + 1) * LANES]) for d in (0, GROUPS // 2)]
                for o in range(count)
            ]
            for h in range(2):
                for o in range(count):
                    for y, side, d in ((lows[o], sides[o][0], 0), (highs[o], sides[o][1], GROUPS // 2)):
                        g = ids_s[p + d, 1 + o, 2 * w + h]
                        y[rows, window(g)] = y[rows, window(g)] + pick(side[h], g)
        return carry

    lax.fori_loop(0, GROUPS // 2, one, 0)


def add_pieces(count, first, takes, lows, highs, out_ref):
    for o in range(count):
        total = None
        for cq in range(4):
            cols = slice(cq * QUARTER, (cq + 1) * QUARTER)
            piece = dot(takes[cq, :, 0:256], lows[o][:, cols]) + dot(takes[cq, :, 256:W], highs[o][:, cols])
            total = piece if total is None else total + piece
        out_ref[:, (first + o) * QUARTER:(first + o + 1) * QUARTER] = total.astype(BF16)


def merge_first_kernel(count, x_ref, out_ref, takes, *rest):
    lows, highs, (ids_v, ids_s, sem) = rest[:count], rest[count:2 * count], rest[2 * count:]
    gather_pieces(count, x_ref, lows, highs, ids_v, ids_s, sem)
    groups = jnp.concatenate([ids_v[p, 0:1, :] for p in range(GROUPS)], axis=0).astype(F32).astype(BF16)
    spread = (((iota((LANES, W), 1) >> 2) & 7) == iota((LANES, W), 0)).astype(F32).astype(BF16)
    each = dot(groups, spread)
    mine = (iota((GROUPS, W), 1) >> 5) == iota((GROUPS, W), 0)
    group = jnp.sum(jnp.where(mine, each, 0.0), axis=0, keepdims=True).astype(I32)
    row, col = iota((256, W), 0), iota((256, W), 1)
    hit = ((row >> 4) == group) & ((row & 3) == (col & 3))
    for cq in range(4):
        takes[cq] = (hit & (((row >> 2) & 3) == cq)).astype(F32).astype(BF16)
    add_pieces(count, 0, takes, lows, highs, out_ref)


def merge_last_kernel(count, x_ref, done, takes, out_ref, *rest):
    lows, highs, (ids_v, ids_s, sem) = rest[:count], rest[count:2 * count], rest[2 * count:]
    out_ref[:, 0:done.shape[1]] = done[...]
    gather_pieces(count, x_ref, lows, highs, ids_v, ids_s, sem)
    add_pieces(count, done.shape[1] // QUARTER, takes, lows, highs, out_ref)


def merge(x, done=None, takes=None):
    count = x.shape[2] // W
    shape = jax.ShapeDtypeStruct
    first = done is None
    earlier = 0 if first else done.shape[1] // QUARTER
    out = shape((256, (earlier + count) * QUARTER), BF16)
    return pl.pallas_call(
        functools.partial(merge_first_kernel if first else merge_last_kernel, count),
        out_shape=(out, shape((4, 256, W), BF16)) if first else out,
        in_specs=[VMEM] * (1 if first else 3),
        out_specs=(VMEM, VMEM) if first else VMEM,
        scratch_shapes=[pltpu.VMEM((GROUPS * CHUNK // 2, GROUPS * TILE), BF16)] * (2 * count)
        + [
            pltpu.VMEM((GROUPS, 8, LANES), I32),
            pltpu.SMEM((GROUPS, 8, LANES), I32),
            pltpu.SemaphoreType.DMA((1,)),
        ],
        compiler_params=params(),
        cost_estimate=pl.CostEstimate(flops=1_000_000_000 * count, bytes_accessed=count << 20, transcendentals=0),
    )(*((x,) if first else (x, done, takes)))


def finish_kernel(order, x_ref, out_h, out_ref, sem):
    row, col = iota((TILE, 256), 0), iota((TILE, 256), 1)
    same = ((row >> 2) == (col >> 4)) & ((row & 3) == (col & 3))
    takes = [(same & (((col >> 2) & 3) == cq)).astype(F32).astype(BF16) for cq in range(4)]
    copies = []
    for n, o in enumerate(order):
        for cq in range(4):
            at = o * 4 * QUARTER + cq * QUARTER
            out_ref[0, :, at:at + QUARTER] = dot(takes[cq], x_ref[:, n * QUARTER:(n + 1) * QUARTER])
        cols = slice(o * 4 * QUARTER, (o + 1) * 4 * QUARTER)
        copies.append(pltpu.make_async_copy(out_ref.at[:, :, cols], out_h.at[:, :, cols], sem.at[n]))
        copies[n].start()
    for copy in copies:
        copy.wait()


def finish(order, x):
    shape = (1, TILE, DENSE)
    return pl.pallas_call(
        functools.partial(finish_kernel, order),
        out_shape=jax.ShapeDtypeStruct(shape, F32),
        in_specs=[VMEM],
        out_specs=ANY,
        scratch_shapes=[pltpu.VMEM(shape, F32), pltpu.SemaphoreType.DMA((len(order),))],
        compiler_params=params(),
    )(x)


def along(block, step):
    count = lax.axis_size("slab")
    route = [(i, (i + step) % count) for i in range(count)]
    return lax.ppermute(block, "slab", route)


def exchange(term):
    return lax.all_to_all(term.reshape(GROUPS, CHUNK, term.shape[1]), "piece", 0, 0)


def hand_over(dense):
    back = lax.all_to_all(dense.reshape(GROUPS, 16, dense.shape[1]), "piece", 0, 0)
    return back.reshape(256, dense.shape[1])


def device_part(fine_tiles, fine_cols, bond_mask, diag_inv, tentative, aggregate, tentative_two, aggregate_two):
    own = pack(fine_tiles, diag_inv, tentative, tentative_two, fine_cols, bond_mask, aggregate, aggregate_two)
    m1, p1 = along(own, 1), along(own, -1)
    slab = lax.axis_index("slab").astype(I32).reshape(1)
    rap, sm, qs, r0, tpt = start_own(own)
    m2 = along(m1, 1)
    p2 = along(p1, -1)
    c, term, part, ra, smo, m1_tail, p1_tail = near(slab, m1, p1, rap, sm, qs, r0, tpt, own)
    m3 = along(m1_tail, 2)
    p3 = along(p1_tail, -2)
    c, term, smm = second(slab, m2, m1, own, part, ra, tpt, c, term)
    got = exchange(term)
    c, term = third(slab, p2, p1, m3, m2, p3, own, sm, smm, smo, ra, tpt, c)
    last = exchange(term)
    done, takes = merge(got)
    level_two = finish((3, 2, 4, 1, 5, 0, 6), hand_over(merge(last, done, takes)))
    return c.reshape(N, TILE, 7 * W), level_two


def solution(mesh):
    both = ("slab", "piece")
    placed = (
        P(both, None, None), P(both, None), P(both, None), P(both, None, None),
        P(both, None, None), P(both), P(both, None, None), P(both),
    )
    return jax.shard_map(
        device_part,
        mesh=mesh,
        in_specs=placed,
        out_specs=(P(both, None, None), P(both, None, None)),
        check_vma=False,
    )
```
